256 devices in a mesh: segment: 32 (over z, y), tensor: 8 (over x, core).
Axes of the slice: x: 4, y: 4, z: 8, core: 2. Of those that a mesh axis runs over, the one named last changes fastest.
Arguments:
- x_in: bfloat16 [128, 8192], P(None, 'tensor'), may hold values from -6 to 6
- neighbour_ids: int32 [512], replicated, may hold values from 0 to 65535
- embed_table: bfloat16 [65536, 896], P(('segment', 'tensor')), may hold values from -6 to 6
- enc_gate: bfloat16 [896, 3584], P(None, 'tensor'), may hold values from -0.1875 to 0.1875
- enc_up: bfloat16 [896, 3584], P(None, 'tensor'), may hold values from -0.1875 to 0.1875
- enc_down: bfloat16 [3584, 896], P('tensor'), may hold values from -0.09375 to 0.09375
- query_weight: bfloat16 [32, 8192, 2048], P('segment', 'tensor'), may hold values from -0.0625 to 0.0625
- key_weight: bfloat16 [32, 896, 2048], P('segment', None, 'tensor'), may hold values from -0.1875 to 0.1875
- value_weight: bfloat16 [32, 896, 2048], P('segment', None, 'tensor'), may hold values from -0.1875 to 0.1875
- out_weight: bfloat16 [32, 2048, 8192], P('segment', None, 'tensor'), may hold values from -0.125 to 0.125
- state_grad: bfloat16 [32, 128, 8192], P('segment', None, 'tensor'), may hold values from -6 to 6
Outputs:
- section_states: bfloat16 [32, 128, 8192], P('segment', None, 'tensor')
- enc_grad: float32 [512, 896], P(('segment', 'tensor'))
The draws below stay inside these ranges and needn't reach their ends.
All inputs are finite; a program needn't handle non-finite values.
Results may differ from the reference program's by a relative error of at most 0.03.
Values may be sent and summed in bfloat16 or wider, within the bound.
No kernel may reach another device: no remote copies, remote signals or barrier semaphores. Data moves between devices by JAX's collectives and lax.ppermute only.
A program may use at most 64 MiB of HBM per device.

```python
import math
import jax
import jax.numpy as jnp
import numpy as np
from jax import lax

D = 8192
HD = 64
DE = 896
FE = 3584
SPAN = 64
SECTIONS = 32
TOKENS = 128
NTOK = 512
HH = 2048
VOCAB = 65536
N_TENSOR = 8


def touch_ends(entries, own_key, smallest, top_value):
    shape = entries.shape
    spot = [jax.random.randint(jax.random.fold_in(own_key, axis), (), 0, shape[axis]) for axis in range(len(shape))]
    entries = entries.at[tuple(spot)].set(smallest)
    longest = shape.index(max(shape))
    spot[longest] = (spot[longest] + 1) % shape[longest]
    return entries.at[tuple(spot)].set(top_value)


def with_spikes(drawn, stream_key, source, target, shards_of, factor):
    owner, partner = [(jnp.arange(drawn.shape[axis_at]) // (drawn.shape[axis_at] // shards_of)).reshape([-1 if axis == axis_at else 1 for axis in range(drawn.ndim)]) for axis_at in (source, target)]
    chosen = jax.random.permutation(stream_key, shards_of)[partner]
    strong = (owner == chosen) | (owner == (partner + shards_of // 2) % shards_of)
    return jnp.where(strong, factor * drawn, drawn)


def steps_of(own_key, shape, cuts, smallest, largest):
    factor_of, own = 1.0, jax.random.fold_in(own_key, 6)
    for dim, blocks in cuts:
        draws = jnp.exp(jax.random.uniform(jax.random.fold_in(own, dim), (blocks,), jnp.float32, smallest / len(cuts), largest / len(cuts)))
        factor_of = factor_of * jnp.repeat(draws, shape[dim] // blocks).reshape([-1 if axis == dim else 1 for axis in range(len(shape))])
    return factor_of


def rank_table(number_of, lean):
    portions = [(1 << 20) // math.isqrt(rank ** lean) + 1 for rank in range(1, number_of + 1)]
    deviation = 1 + sum(portions) // (1 << 30)
    return np.cumsum(np.array([max(1, weight // deviation) for weight in portions]))


def ranked(rng, shape, count, slope):
    listing = rank_table(count, slope)
    ticket = jax.random.randint(jax.random.fold_in(rng, 1), shape, 0, int(listing[count - 1]))
    grade = jnp.searchsorted(jnp.asarray(listing, jnp.int32), ticket, side="right")
    return jax.random.permutation(jax.random.fold_in(rng, 2), count)[grade].astype(jnp.int32)


def centred(stream_key, extent, deviation, bound, cuts=(), kind=jnp.bfloat16):
    entries = deviation * jax.random.normal(stream_key, extent, jnp.float32)
    if cuts:
        entries = entries * steps_of(stream_key, extent, cuts, -0.22, 0.18)
    return jnp.clip(entries, -bound, bound).astype(kind)


def noise_with(rng, extent, width, reach, cuts, heavy, dtype=jnp.bfloat16):
    values = width * jax.random.normal(rng, extent, jnp.float32)
    if cuts:
        values = values * steps_of(rng, extent, cuts, -0.22, 0.18)
    return jnp.clip(with_spikes(values, jax.random.fold_in(rng, 3), *heavy), -reach, reach).astype(dtype)


def setup_inputs(seed: int = 0) -> dict:
    keys = jax.random.split(jax.random.key(seed), 12)
    x_in = centred(keys[0], (TOKENS, D), 1.0, 6.0, ((1, 8),))
    neighbour_ids = touch_ends(ranked(keys[1], (NTOK,), VOCAB, 2), jax.random.fold_in(keys[1], 3), 0, VOCAB - 1).astype(jnp.int32)
    embed_table = centred(keys[2], (VOCAB, DE), 1.0, 6.0, ((0, 256),))
    enc_gate = centred(keys[3], (DE, FE), DE ** -0.5, 0.1875, ((1, 8),))
    enc_up = centred(keys[4], (DE, FE), DE ** -0.5, 0.1875, ((1, 8),))
    enc_down = centred(keys[5], (FE, DE), FE ** -0.5, 0.09375, ((0, 8),))
    query_weight = centred(keys[6], (SECTIONS, D, HH), D ** -0.5, 0.0625, ((0, 32), (1, 8)))
    key_weight = centred(keys[7], (SECTIONS, DE, HH), DE ** -0.5, 0.1875, ((0, 32), (2, 8)))
    value_weight = centred(keys[8], (SECTIONS, DE, HH), DE ** -0.5, 0.1875, ((0, 32), (2, 8)))
    out_weight = centred(keys[9], (SECTIONS, HH, D), HH ** -0.5, 0.125, ((0, 32), (2, 8)))
    state_grad = noise_with(keys[10], (SECTIONS, TOKENS, D), 1.0, 6.0, ((0, 32), (2, 8)), (0, 1, 32, 2.75))
    return {"x_in": x_in, "neighbour_ids": neighbour_ids, "embed_table": embed_table, "enc_gate": enc_gate, "enc_up": enc_up, "enc_down": enc_down, "query_weight": query_weight, "key_weight": key_weight, "value_weight": value_weight, "out_weight": out_weight, "state_grad": state_grad}


EPSILON = 1e-06
SCORE_GAIN = 2.0

def normalize_heads(block_in):
    return block_in * lax.rsqrt(lax.optimization_barrier(jnp.mean(block_in * block_in, axis=-1, keepdims=True)) + EPSILON)

def attend(query_rows, key_rows, value_rows):
    feat_width = query_rows.shape[-1]
    head_count = feat_width // HD
    span_count = query_rows.shape[0] // SPAN
    query_heads = normalize_heads(query_rows.reshape(span_count, SPAN, head_count, HD))
    key_heads = normalize_heads(key_rows.reshape(span_count, -1, head_count, HD))
    value_heads = value_rows.reshape(span_count, -1, head_count, HD)
    scores = jnp.einsum('cihd,cjhd->chij', query_heads, key_heads, precision=lax.Precision.HIGHEST)
    scores = scores * (SCORE_GAIN / math.sqrt(HD))
    weights = jnp.exp(scores)
    weights = weights / lax.optimization_barrier(jnp.sum(weights, axis=-1, keepdims=True))
    output = jnp.einsum('chij,cjhd->cihd', weights, value_heads, precision=lax.Precision.HIGHEST)
    return output.reshape(span_count * SPAN, feat_width)

def encoder_partial(tok_rows, enc_gate, enc_up, enc_down):
    gate_proj = jnp.dot(tok_rows, enc_gate, preferred_element_type=jnp.float32)
    up_proj = jnp.dot(tok_rows, enc_up, preferred_element_type=jnp.float32)
    hidden = (jax.nn.silu(gate_proj) * up_proj).astype(jnp.bfloat16)
    return jnp.dot(hidden, enc_down, preferred_element_type=jnp.float32)

def finish(tok_rows, summed):
    resid = tok_rows.astype(jnp.float32) + summed
    return (resid * lax.rsqrt(lax.optimization_barrier(jnp.mean(resid * resid, axis=-1, keepdims=True)) + EPSILON)).astype(jnp.bfloat16)

def reference(x_in, neighbour_ids, embed_table, enc_gate, enc_up, enc_down, query_weight, key_weight, value_weight, out_weight, state_grad):
    embedded = embed_table[neighbour_ids]
    encodings = finish(embedded, encoder_partial(embedded, enc_gate, enc_up, enc_down))
    block_width = D // N_TENSOR
    x_float = x_in.astype(jnp.float32)

    def section(running, weights_in):
        w_query, w_key, w_value, w_out, grad_now = weights_in
        pieces = []
        for block_idx in range(N_TENSOR):
            lower = block_idx * block_width
            pieces.append(jnp.dot(x_in[:, lower:lower + block_width], w_query[lower:lower + block_width], preferred_element_type=jnp.float32))
        stacked = lax.optimization_barrier(jnp.stack(pieces).astype(jnp.bfloat16))
        queries = lax.optimization_barrier(jnp.sum(stacked.astype(jnp.float32), axis=0))
        key_rows = jnp.dot(encodings, w_key, preferred_element_type=jnp.float32)
        value_rows = jnp.dot(encodings, w_value, preferred_element_type=jnp.float32)
        attended = attend(queries, key_rows, value_rows).astype(jnp.bfloat16)
        running = running + jnp.dot(attended, w_out, preferred_element_type=jnp.float32)
        updated = (x_float + running).astype(jnp.bfloat16)
        head_grad = jnp.dot(grad_now, w_out.T, preferred_element_type=jnp.float32)
        _, pull_back = jax.vjp(lambda k_in, v_in: attend(queries, k_in, v_in), key_rows, value_rows)
        key_grad, value_grad = pull_back(head_grad)
        term = jnp.dot(key_grad.astype(jnp.bfloat16), w_key.T, preferred_element_type=jnp.float32)
        term = term + jnp.dot(value_grad.astype(jnp.bfloat16), w_value.T, preferred_element_type=jnp.float32)
        return (running, (updated, term))
    start = jnp.zeros(x_in.shape, jnp.float32)
    _, outputs = lax.scan(section, start, (query_weight, key_weight, value_weight, out_weight, state_grad))
    section_states, terms = outputs
    return (section_states, lax.optimization_barrier(jnp.sum(terms, axis=0)))
```

```python
import math

import jax
import jax.numpy as jnp
from jax import lax
from jax.experimental import pallas as pl
from jax.experimental.pallas import tpu as pltpu
from jax.sharding import Mesh
from jax.sharding import PartitionSpec as P

HD = 64
SPAN = 64
Z, Y, X, C = "segment_0", "segment_1", "tensor_0", "tensor_1"
SEGMENT = (Z, Y)
TENSOR = (X, C)
SEGMENT_TENSOR = (Z, Y, X, C)

EPSILON = 1e-06
SCORE_GAIN = 2.0
F32 = jnp.float32
BF16 = jnp.bfloat16


NT = (((1,), (1,)), ((), ()))
TN = (((0,), (0,)), ((), ()))
NN = (((1,), (0,)), ((), ()))


def swap(value, axis, k):
    size = lax.axis_size(axis)
    return lax.ppermute(value, axis, [(i, i ^ k) for i in range(size)])


def dot(lhs, rhs, dims=NN):
    return lax.dot_general(lhs, rhs, dims, preferred_element_type=F32)


def halves(value):
    high = value.astype(BF16)
    return high, (value - high.astype(F32)).astype(BF16)


def head_of(shape, dim):
    return lax.broadcasted_iota(jnp.int32, shape, dim) // HD


def head_mean(value):
    width = value.shape[-1]
    same = head_of((width, width), 0) == head_of((width, width), 1)
    mean = jnp.where(same, 1.0 / HD, 0.0).astype(BF16)
    high, low = halves(value)
    return dot(high, mean) + dot(low, mean)


def by_head(rows):
    heads = rows.shape[-1] // HD
    which = head_of(rows.shape, 1)
    return jnp.concatenate([jnp.where(which == h, rows, 0.0) for h in range(heads)], axis=0)


def project_kernel(_, x_ref, wq_ref, grad_ref, wo_ref, out_ref):
    out_ref[0, 0] = dot(x_ref[...], wq_ref[...]).astype(BF16)
    out_ref[0, 1] = dot(grad_ref[...], wo_ref[...], NT).astype(BF16)


def project(index, x_in, w_query, grad, w_out, other_core):
    tokens, depth = x_in.shape
    blocks = w_query.shape[1] // 256 // 2
    return pl.pallas_call(
        project_kernel,
        out_shape=jax.ShapeDtypeStruct((blocks, 2, tokens, 256), BF16),
        grid_spec=pltpu.PrefetchScalarGridSpec(
            num_scalar_prefetch=1,
            grid=(blocks,),
            in_specs=[
                pl.BlockSpec((tokens, depth), lambda k, t: (0, 0)),
                pl.BlockSpec((depth, 256), lambda k, t: (0, t[0] ^ (2 * k + other_core))),
                pl.BlockSpec((tokens, depth), lambda k, t: (0, 0)),
                pl.BlockSpec((256, depth), lambda k, t: (t[0] ^ (2 * k + other_core), 0)),
            ],
            out_specs=pl.BlockSpec((1, 2, tokens, 256), lambda k, t: (k, 0, 0, 0)),
        ),
        cost_estimate=pl.CostEstimate(
            flops=4 * tokens * depth * 256 * blocks,
            bytes_accessed=4 * depth * 256 * blocks,
            transcendentals=0,
        ),
        name="project",
    )(index, x_in, w_query, grad, w_out)


def attend_kernel(own_ref, oth_ref, wk_ref, wv_ref, q0, q1, q2, q3,
                  att_ref, key_ref, val_ref, weight_ref, qhat_ref):
    wk = wk_ref[...]
    wv = wv_ref[...]
    query = sum(q[0].astype(F32) for q in (q0, q1, q2, q3))
    query = query * lax.rsqrt(head_mean(query * query) + EPSILON)
    qhat_ref[...] = query.astype(BF16)
    for span in range(2):
        enc = jnp.concatenate([own_ref[span], oth_ref[span]], axis=0)
        key = dot(enc, wk)
        value = dot(enc, wv).astype(BF16)
        key_ref[span] = key
        val_ref[span] = value
        khat = key * lax.rsqrt(head_mean(key * key) + EPSILON)
        q_high, q_low = halves(by_head(query[span * SPAN : (span + 1) * SPAN]))
        k_high, k_low = halves(khat)
        score = dot(q_high, k_high, NT) + dot(q_high, k_low, NT) + dot(q_low, k_high, NT)
        weight = jnp.exp(score * (SCORE_GAIN / math.sqrt(HD)))
        weight = weight / jnp.sum(weight, axis=-1, keepdims=True)
        weight_ref[span] = weight
        mixed = dot(weight.astype(BF16), value)
        which = head_of((SPAN, 256), 1)
        out = jnp.zeros((SPAN, 256), F32)
        for h in range(4):
            out = jnp.where(which == h, mixed[h * SPAN : (h + 1) * SPAN], out)
        att_ref[span * SPAN : (span + 1) * SPAN] = out.astype(BF16)


def whole(shape):
    return pl.BlockSpec(shape, lambda: (0,) * len(shape))


def attend(own, oth, w_key, w_value, pieces):
    depth = w_key.shape[0]
    piece = whole((2, 128, 256))
    shapes = [((128, 256), BF16), ((2, 256, 256), F32), ((2, 256, 256), BF16),
              ((2, 256, 256), F32), ((128, 256), BF16)]
    return pl.pallas_call(
        attend_kernel,
        out_shape=[jax.ShapeDtypeStruct(*s) for s in shapes],
        in_specs=[whole((2, 128, depth))] * 2 + [whole((depth, 256))] * 2 + [piece] * 4,
        out_specs=[whole(s[0]) for s in shapes],
        cost_estimate=pl.CostEstimate(
            flops=4 * 512 * depth * 256, bytes_accessed=4 * 512 * depth, transcendentals=131072
        ),
        name="attend",
    )(own, oth, w_key, w_value, *pieces)


def backward_kernel(x_ref, h0, h1, h2, h3, key_ref, val_ref, weight_ref, qhat_ref, wk_ref, wv_ref,
                    keep_ref, send_ref):
    wk = wk_ref[...]
    wv = wv_ref[...]
    grad = sum(h[1].astype(F32) for h in (h0, h1, h2, h3))
    for span in range(2):
        rows = slice(span * SPAN, (span + 1) * SPAN)
        d_out = by_head(grad[rows]).astype(BF16)
        q_rows = by_head(qhat_ref[rows].astype(F32)).astype(BF16)
        weight = weight_ref[span]
        value = val_ref[span]
        d_value = dot(weight.astype(BF16), d_out, TN).astype(BF16)
        d_weight = dot(d_out, value, NT)
        d_score = weight * (d_weight - jnp.sum(weight * d_weight, axis=-1, keepdims=True))
        d_khat = dot(d_score.astype(BF16), q_rows, TN) * (SCORE_GAIN / math.sqrt(HD))
        key = key_ref[span]
        scale = lax.rsqrt(head_mean(key * key) + EPSILON)
        khat = key * scale
        d_key = (scale * (d_khat - khat * head_mean(d_khat * khat))).astype(BF16)
        term = dot(d_key, wk, NT) + dot(d_value, wv, NT)
        for block in range(4):
            place = x_ref[0] ^ block
            keep_ref[place, span] = term[block * 32 : (block + 1) * 32].astype(BF16)
            send_ref[place, span] = term[128 + block * 32 : 128 + (block + 1) * 32].astype(BF16)


def backward(x_index, pieces, saved, w_key, w_value):
    depth = w_key.shape[0]
    piece = whole((2, 128, 256))
    key, value, weight, qhat = saved
    return pl.pallas_call(
        backward_kernel,
        out_shape=[jax.ShapeDtypeStruct((4, 2, 32, depth), BF16)] * 2,
        in_specs=[pl.BlockSpec(memory_space=pltpu.SMEM)] + [piece] * 4
        + [whole((2, 256, 256))] * 3 + [whole((128, 256))] + [whole((depth, 256))] * 2,
        out_specs=[whole((4, 2, 32, depth))] * 2,
        cost_estimate=pl.CostEstimate(
            flops=4 * 512 * depth * 256, bytes_accessed=4 * 512 * depth, transcendentals=0
        ),
        name="backward",
    )(x_index, *pieces, key, value, weight, qhat, w_key, w_value)


def output_first_kernel(_, att_ref, wo_ref, out_ref):
    part = dot(att_ref[0], wo_ref[...])
    step = pl.program_id(0)

    @pl.when(step == 0)
    def _():
        out_ref[...] = part

    @pl.when(step > 0)
    def _():
        out_ref[...] += part


def output_second_kernel(_, att_ref, wo_ref, base_ref, out_ref, acc_ref):
    part = dot(att_ref[0], wo_ref[...])
    step = pl.program_id(0)

    @pl.when(step == 0)
    def _():
        acc_ref[...] = base_ref[...] + part

    @pl.when(step > 0)
    def _():
        acc_ref[...] += part

    @pl.when(step == pl.num_programs(0) - 1)
    def _():
        for block in range(16):
            for half in range(2):
                out_ref[2 * block + half] = acc_ref[
                    block * 8 : (block + 1) * 8, half * 512 : (half + 1) * 512
                ].astype(BF16)


def output(index, att, w_out, base):
    width = w_out.shape[1]
    second = base is not None
    other_core = int(second)
    in_specs = [
        pl.BlockSpec((1, 128, 256), lambda k, t: (k, 0, 0)),
        pl.BlockSpec((256, width), lambda k, t: (t[0] ^ (2 * k + other_core), 0)),
    ]
    if second:
        in_specs.append(pl.BlockSpec((128, width), lambda k, t: (0, 0)))
        shape, dtype = (32, 8, 512), BF16
    else:
        shape, dtype = (128, width), F32
    return pl.pallas_call(
        output_second_kernel if second else output_first_kernel,
        out_shape=jax.ShapeDtypeStruct(shape, dtype),
        grid_spec=pltpu.PrefetchScalarGridSpec(
            num_scalar_prefetch=1,
            grid=(4,),
            in_specs=in_specs,
            out_specs=pl.BlockSpec(shape, lambda k, t: (0,) * len(shape)),
            scratch_shapes=[pltpu.VMEM((128, width), F32)] if second else [],
        ),
        cost_estimate=pl.CostEstimate(
            flops=2 * 128 * 1024 * width, bytes_accessed=2 * 1024 * width, transcendentals=0
        ),
        name="output",
    )(index, att, w_out, *([base] if second else []))


def scan_kernel(index_ref, x_ref, piece_ref, out_ref):
    where = index_ref[0]
    row = pl.multiple_of((where // 2) * 8, 8)
    column = pl.multiple_of((where % 2) * 512, 512)
    running = jnp.zeros((8, 512), F32)
    start = x_ref[pl.ds(row, 8), pl.ds(column, 512)].astype(F32)
    for section in range(piece_ref.shape[0]):
        running = running + piece_ref[section].astype(F32)
        out_ref[section] = (start + running).astype(BF16)


def scan(index, x_in, pieces):
    return pl.pallas_call(
        scan_kernel,
        out_shape=jax.ShapeDtypeStruct(pieces.shape, BF16),
        in_specs=[pl.BlockSpec(memory_space=pltpu.SMEM), whole(x_in.shape), whole(pieces.shape)],
        out_specs=whole(pieces.shape),
        cost_estimate=pl.CostEstimate(flops=262144, bytes_accessed=786432, transcendentals=0),
        name="scan",
    )(index, x_in, pieces)


def gathered_sum(value, keep=None):
    parts = [swap(value, X, k) for k in (1, 2, 3)]
    total = value.astype(F32) if keep is None else keep
    return total + sum(p.astype(F32) for p in parts)


def body(
    x_in,
    neighbour_ids,
    embed_table,
    enc_gate,
    enc_up,
    enc_down,
    query_weight,
    key_weight,
    value_weight,
    out_weight,
    state_grad,
):
    sections = lax.axis_size(SEGMENT)
    section = lax.axis_index(SEGMENT).astype(jnp.int32)
    tensor = lax.axis_index(TENSOR).astype(jnp.int32)
    core = lax.axis_index(C)
    x_index = lax.axis_index(X).astype(jnp.int32)[None]
    t_index = tensor[None]
    s_index = section[None]
    vocab_rows, depth = embed_table.shape
    first_row = (section * lax.axis_size(TENSOR) + tensor) * vocab_rows

    local = (neighbour_ids - first_row).reshape(2, 16, 4, 2, 2).transpose(3, 0, 2, 1, 4).reshape(2, 256)
    rows = jnp.arange(vocab_rows, dtype=jnp.int32)[None, :]

    def lookup(which):
        ids = lax.dynamic_index_in_dim(local, which, 0, keepdims=False)
        return dot((ids[:, None] == rows).astype(BF16), embed_table).astype(BF16)

    arrived = swap(lookup(1 - core), C, 1)
    paired = (lookup(core) + arrived).reshape(sections, 8, depth)
    own = lax.all_to_all(paired, SEGMENT, 0, 0, tiled=True)
    own = jnp.sum(own.astype(F32), axis=0).astype(BF16)

    w_query, w_key, w_value, w_out = query_weight[0], key_weight[0], value_weight[0], out_weight[0]
    grad_local = state_grad[0]
    sent = swap(project(t_index, x_in, w_query, grad_local, w_out, 1), C, 1)
    kept = project(t_index, x_in, w_query, grad_local, w_out, 0)
    both = (kept.astype(F32) + sent.astype(F32)).astype(BF16)
    pieces = [both[0]] + [swap(both[k], X, k) for k in (1, 2, 3)]

    own = gathered_sum(own).astype(BF16)
    tok_rows = jnp.concatenate([own, swap(own, C, 1)], axis=0)
    gate = dot(tok_rows, enc_gate)
    hidden = (jax.nn.silu(gate) * dot(tok_rows, enc_up)).astype(BF16)
    partial = dot(hidden, enc_down)
    partial = (partial[:8] + swap(partial[8:].astype(BF16), C, 1).astype(F32)).astype(BF16)
    resid = own.astype(F32) + gathered_sum(partial)
    encoding = (
        resid * lax.rsqrt(jnp.mean(resid * resid, axis=-1, keepdims=True) + EPSILON)
    ).astype(BF16)
    enc_own = lax.all_to_all(
        jnp.broadcast_to(encoding[None], (sections, 8, depth)), SEGMENT, 0, 0, tiled=True
    ).reshape(2, 128, depth)
    enc_oth = swap(enc_own, C, 1)

    att, *saved = attend(enc_own, enc_oth, w_key, w_value, pieces)
    atts = jnp.stack([att] + [swap(att, X, k) for k in (1, 2, 3)])
    keep, send = backward(x_index, pieces, saved, w_key, w_value)
    atts_other = swap(atts, C, 1)
    first = output(t_index, atts, w_out, None)
    contribution = output(t_index, atts_other, w_out, first)
    contributions = lax.all_to_all(contribution, SEGMENT, 0, 0, tiled=True)
    states = scan(s_index, x_in, contributions)
    states = lax.all_to_all(states, SEGMENT, 0, 0, tiled=True)
    states = states.reshape(16, 2, 8, 512).transpose(0, 2, 1, 3).reshape(1, 128, 1024)

    terms = (keep.astype(F32) + swap(send, C, 1).astype(F32)).astype(BF16)
    term = terms[0].astype(F32) + sum(swap(terms[k], X, k).astype(F32) for k in (1, 2, 3))
    term = term.astype(BF16).reshape(sections, 2, depth)
    enc_grad = jnp.sum(lax.all_to_all(term, SEGMENT, 0, 0, tiled=True).astype(F32), axis=0)
    return states, enc_grad


def solution(mesh):
    split = Mesh(mesh.devices.reshape(8, 4, 4, 2), SEGMENT_TENSOR)
    return jax.shard_map(
        body,
        mesh=split,
        in_specs=(
            P(None, TENSOR),
            P(),
            P(SEGMENT_TENSOR, None),
            P(None, TENSOR),
            P(None, TENSOR),
            P(TENSOR, None),
            P(SEGMENT, TENSOR, None),
            P(SEGMENT, None, TENSOR),
            P(SEGMENT, None, TENSOR),
            P(SEGMENT, None, TENSOR),
            P(SEGMENT, None, TENSOR),
        ),
        out_specs=(P(SEGMENT, None, TENSOR), P(SEGMENT_TENSOR, None)),
        check_vma=False,
    )
```

```python
import functools
import math

import jax
import jax.numpy as jnp
from jax import lax
from jax.experimental import pallas as pl
from jax.experimental.pallas import tpu as pltpu
from jax.sharding import Mesh
from jax.sharding import PartitionSpec as P


HD = 64
SPAN = 64
Z, Y, X, C = "segment_0", "segment_1", "tensor_0", "tensor_1"
SEGMENT = (Z, Y)
TENSOR = (X, C)
SEGMENT_TENSOR = (Z, Y, X, C)

EPSILON = 1e-06
SCORE_GAIN = 2.0
F32 = jnp.float32
BF16 = jnp.bfloat16


NT = (((1,), (1,)), ((), ()))
TN = (((0,), (0,)), ((), ()))
NN = (((1,), (0,)), ((), ()))

PARAMS = pltpu.CompilerParams(vmem_limit_bytes=24 << 20)


def swap(value, axis, k):
    size = lax.axis_size(axis)
    return lax.ppermute(value, axis, [(i, i ^ k) for i in range(size)])


def dot(lhs, rhs, dims=NN):
    return lax.dot_general(lhs, rhs, dims, preferred_element_type=F32)


def halves(value):
    high = value.astype(BF16)
    return high, (value - high.astype(F32)).astype(BF16)


def head_of(shape, dim):
    return lax.broadcasted_iota(jnp.int32, shape, dim) // HD


def head_mean(value):
    width = value.shape[-1]
    same = head_of((width, width), 0) == head_of((width, width), 1)
    mean = jnp.where(same, 1.0 / HD, 0.0).astype(BF16)
    high, low = halves(value)
    return dot(high, mean) + dot(low, mean)


def by_head(rows):
    heads = rows.shape[-1] // HD
    which = head_of(rows.shape, 1)
    return jnp.concatenate([jnp.where(which == h, rows, 0.0) for h in range(heads)], axis=0)


def project_kernel(index_ref, x_ref, wq_ref, grad_ref, wo_ref, out_ref, q_buf, o_buf, sem, *, other_core):
    copies = []
    for k in range(4):
        start = pl.multiple_of((index_ref[0] ^ (2 * k + other_core)) * 256, 256)
        copies.append(
            (
                pltpu.make_async_copy(wq_ref.at[:, pl.ds(start, 256)], q_buf.at[k], sem.at[0, k]),
                pltpu.make_async_copy(wo_ref.at[pl.ds(start, 256), :], o_buf.at[k], sem.at[1, k]),
            )
        )
        for copy in copies[k]:
            copy.start()
    for k in range(4):
        for copy in copies[k]:
            copy.wait()
        out_ref[k, 0] = dot(x_ref[...], q_buf[k]).astype(BF16)
        out_ref[k, 1] = dot(grad_ref[...], o_buf[k], NT).astype(BF16)


def project(index, x_in, w_query, grad, w_out, other_core):
    tokens, depth = x_in.shape
    shape = (4, 2, tokens, 256)
    anywhere = pl.BlockSpec(memory_space=pltpu.HBM)
    return pl.pallas_call(
        functools.partial(project_kernel, other_core=other_core),
        out_shape=jax.ShapeDtypeStruct(shape, BF16),
        in_specs=[
            pl.BlockSpec(memory_space=pltpu.SMEM),
            whole((tokens, depth)),
            anywhere,
            whole((tokens, depth)),
            anywhere,
        ],
        out_specs=whole(shape),
        scratch_shapes=[
            pltpu.VMEM((4, depth, 256), BF16),
            pltpu.VMEM((4, 256, depth), BF16),
            pltpu.SemaphoreType.DMA((2, 4)),
        ],
        cost_estimate=pl.CostEstimate(
            flops=16 * tokens * depth * 256, bytes_accessed=16 * depth * 256, transcendentals=0
        ),
        compiler_params=PARAMS,
        name="project",
    )(index, x_in, w_query, grad, w_out)


def attend_kernel(own_ref, oth_ref, wk_ref, wv_ref, heads_ref, att_ref,
                  key_ref, val_ref, weight_ref, qhat_ref):
    wk = wk_ref[...]
    wv = wv_ref[...]
    query = heads_ref[0]
    query = query * lax.rsqrt(head_mean(query * query) + EPSILON)
    qhat_ref[...] = query.astype(BF16)
    for span in range(2):
        enc = jnp.concatenate([own_ref[span], oth_ref[span]], axis=0)
        key = dot(enc, wk)
        value = dot(enc, wv).astype(BF16)
        key_ref[span] = key
        val_ref[span] = value
        khat = key * lax.rsqrt(head_mean(key * key) + EPSILON)
        q_high, q_low = halves(by_head(query[span * SPAN : (span + 1) * SPAN]))
        k_high, k_low = halves(khat)
        score = dot(q_high, k_high, NT) + dot(q_high, k_low, NT) + dot(q_low, k_high, NT)
        weight = jnp.exp(score * (SCORE_GAIN / math.sqrt(HD)))
        weight = weight / jnp.sum(weight, axis=-1, keepdims=True)
        weight_ref[span] = weight
        mixed = dot(weight.astype(BF16), value)
        which = head_of((SPAN, 256), 1)
        out = jnp.zeros((SPAN, 256), F32)
        for h in range(4):
            out = jnp.where(which == h, mixed[h * SPAN : (h + 1) * SPAN], out)
        att_ref[span * SPAN : (span + 1) * SPAN] = out.astype(BF16)


def whole(shape):
    return pl.BlockSpec(shape, lambda: (0,) * len(shape))


def attend(own, oth, w_key, w_value, heads):
    depth = w_key.shape[0]
    piece = whole((2, 128, 256))
    shapes = [((128, 256), BF16), ((2, 256, 256), F32), ((2, 256, 256), BF16),
              ((2, 256, 256), F32), ((128, 256), BF16)]
    return pl.pallas_call(
        attend_kernel,
        out_shape=[jax.ShapeDtypeStruct(*s) for s in shapes],
        in_specs=[whole((2, 128, depth))] * 2 + [whole((depth, 256))] * 2 + [piece],
        out_specs=[whole(s[0]) for s in shapes],
        cost_estimate=pl.CostEstimate(
            flops=4 * 512 * depth * 256, bytes_accessed=4 * 512 * depth, transcendentals=131072
        ),
        compiler_params=PARAMS,
        name="attend",
    )(own, oth, w_key, w_value, heads)


def backward_kernel(x_ref, heads_ref, key_ref, val_ref, weight_ref, qhat_ref, wk_ref, wv_ref,
                    keep_ref, send_ref):
    wk = wk_ref[...]
    wv = wv_ref[...]
    grad = heads_ref[1]
    for span in range(2):
        rows = slice(span * SPAN, (span + 1) * SPAN)
        d_out = by_head(grad[rows]).astype(BF16)
        q_rows = by_head(qhat_ref[rows].astype(F32)).astype(BF16)
        weight = weight_ref[span]
        value = val_ref[span]
        d_value = dot(weight.astype(BF16), d_out, TN).astype(BF16)
        d_weight = dot(d_out, value, NT)
        d_score = weight * (d_weight - jnp.sum(weight * d_weight, axis=-1, keepdims=True))
        d_khat = dot(d_score.astype(BF16), q_rows, TN) * (SCORE_GAIN / math.sqrt(HD))
        key = key_ref[span]
        scale = lax.rsqrt(head_mean(key * key) + EPSILON)
        khat = key * scale
        d_key = (scale * (d_khat - khat * head_mean(d_khat * khat))).astype(BF16)
        term = dot(d_key, wk, NT) + dot(d_value, wv, NT)
        for block in range(4):
            place = x_ref[0] ^ block
            keep_ref[place, span] = term[block * 32 : (block + 1) * 32].astype(BF16)
            send_ref[place, span] = term[128 + block * 32 : 128 + (block + 1) * 32].astype(BF16)


def backward(x_index, heads, saved, w_key, w_value):
    depth = w_key.shape[0]
    piece = whole((2, 128, 256))
    key, value, weight, qhat = saved
    return pl.pallas_call(
        backward_kernel,
        out_shape=[jax.ShapeDtypeStruct((4, 2, 32, depth), BF16)] * 2,
        in_specs=[pl.BlockSpec(memory_space=pltpu.SMEM)] + [piece]
        + [whole((2, 256, 256))] * 3 + [whole((128, 256))] + [whole((depth, 256))] * 2,
        out_specs=[whole((4, 2, 32, depth))] * 2,
        cost_estimate=pl.CostEstimate(
            flops=4 * 512 * depth * 256, bytes_accessed=4 * 512 * depth, transcendentals=0
        ),
        compiler_params=PARAMS,
        name="backward",
    )(x_index, heads, key, value, weight, qhat, w_key, w_value)


def output_kernel(index_ref, att_ref, wo_ref, *refs, other_core):
    base_ref = refs[0] if other_core else None
    out_ref, buf_ref, sem = refs[-3:]
    copies = []
    for k in range(4):
        row = pl.multiple_of((index_ref[0] ^ (2 * k + other_core)) * 256, 256)
        copies.append(
            pltpu.make_async_copy(
                wo_ref.at[pl.ds(row, 256), :], buf_ref.at[pl.ds(k * 256, 256), :], sem.at[k]
            )
        )
        copies[k].start()
    att = jnp.concatenate([att_ref[k] for k in range(4)], axis=1)
    for copy in copies:
        copy.wait()
    for column in range(4):
        lanes = slice(column * 256, (column + 1) * 256)
        part = dot(att, buf_ref[:, lanes])
        if not other_core:
            out_ref[:, lanes] = part
            continue
        part = (base_ref[:, lanes] + part).astype(BF16)
        half, lane = divmod(column * 256, 512)
        for block in range(16):
            out_ref[2 * block + half, :, lane : lane + 256] = part[block * 8 : (block + 1) * 8]


def output(index, att, w_out, base):
    width = w_out.shape[1]
    second = base is not None
    shape, dtype = ((32, 8, 512), BF16) if second else ((128, width), F32)
    return pl.pallas_call(
        functools.partial(output_kernel, other_core=int(second)),
        out_shape=jax.ShapeDtypeStruct(shape, dtype),
        in_specs=[
            pl.BlockSpec(memory_space=pltpu.SMEM),
            whole((4, 128, 256)),
            pl.BlockSpec(memory_space=pl.ANY),
        ]
        + ([whole((128, width))] if second else []),
        out_specs=whole(shape),
        scratch_shapes=[pltpu.VMEM((1024, width), BF16), pltpu.SemaphoreType.DMA((4,))],
        cost_estimate=pl.CostEstimate(
            flops=2 * 128 * 1024 * width, bytes_accessed=2 * 1024 * width, transcendentals=0
        ),
        compiler_params=PARAMS,
        name="output",
    )(index, att, w_out, *([base] if second else []))


def lookup_kernel(index_ref, ids_ref, table_ref, own_ref, oth_ref):
    core = index_ref[0]
    ids = ids_ref[...] - index_ref[1]
    depth, count = table_ref.shape[0], ids.shape[1]
    hot = jnp.where(lax.broadcasted_iota(jnp.int32, (depth, count), 0) == ids, 1.0, 0.0).astype(BF16)
    source = lax.broadcasted_iota(jnp.int32, (count, count // 2), 0)
    place = lax.broadcasted_iota(jnp.int32, (count, count // 2), 1)
    token = ((place >> 7) << 8) + (((place >> 1) & 15) << 4) + (((place >> 5) & 3) << 2) + (place & 1)
    for out_ref, which in ((oth_ref, 1 - core), (own_ref, core)):
        pick = jnp.where(source == token + 2 * which, 1.0, 0.0).astype(BF16)
        out_ref[...] = dot(dot(hot, pick).astype(BF16), table_ref[...], TN).astype(BF16)


def lookup(index, ids, table):
    shape = (ids.shape[1] // 2, table.shape[1])
    return pl.pallas_call(
        lookup_kernel,
        out_shape=[jax.ShapeDtypeStruct(shape, BF16)] * 2,
        in_specs=[pl.BlockSpec(memory_space=pltpu.SMEM), whole(ids.shape), whole(table.shape)],
        out_specs=[whole(shape)] * 2,
        cost_estimate=pl.CostEstimate(
            flops=4 * 256 * 256 * 896, bytes_accessed=4 * 512 * 896, transcendentals=0
        ),
        compiler_params=PARAMS,
        name="lookup",
    )(index, ids, table)


def encode_kernel(own_ref, oth_ref, gate_ref, up_ref, down_ref, keep_ref, send_ref):
    rows = jnp.concatenate([own_ref[...], oth_ref[...]], axis=0)
    gate = dot(rows, gate_ref[...], NT)
    hidden = (gate / (1.0 + jnp.exp(-gate)) * dot(rows, up_ref[...], NT)).astype(BF16)
    partial = dot(hidden, down_ref[...])
    keep_ref[...] = partial[:8]
    send_ref[...] = partial[8:].astype(BF16)


def encode(own, oth, enc_gate, enc_up, enc_down):
    operands = (own, oth, enc_gate.T, enc_up.T, enc_down)
    return pl.pallas_call(
        encode_kernel,
        out_shape=[jax.ShapeDtypeStruct(own.shape, F32), jax.ShapeDtypeStruct(own.shape, BF16)],
        in_specs=[whole(o.shape) for o in operands],
        out_specs=[whole(own.shape)] * 2,
        cost_estimate=pl.CostEstimate(
            flops=6 * 16 * 896 * 448, bytes_accessed=6 * 896 * 448, transcendentals=8192
        ),
        compiler_params=PARAMS,
        name="encode",
    )(*operands)


def pack_kernel(t0, t1, t2, t3, out_ref, term_ref, wide_ref):
    for chunk in range(7):
        lanes = slice(chunk * 128, (chunk + 1) * 128)
        term_ref[chunk] = sum(t[:, lanes].astype(F32) for t in (t0, t1, t2, t3))
    wide_ref[...] = jnp.zeros_like(wide_ref)
    for chunk in range(7):
        for row in range(2):
            wide_ref[:, chunk, row * 128 : (row + 1) * 128] = term_ref[
                chunk, pl.ds(row, 32, stride=2), :
            ]
    out_ref[...] = wide_ref[...].astype(BF16)


def pack(terms):
    shape = (32, 8, 256)
    return pl.pallas_call(
        pack_kernel,
        out_shape=jax.ShapeDtypeStruct(shape, BF16),
        in_specs=[whole((64, 896))] * 4,
        out_specs=whole(shape),
        scratch_shapes=[pltpu.VMEM((7, 64, 128), F32), pltpu.VMEM(shape, F32)],
        cost_estimate=pl.CostEstimate(flops=262144, bytes_accessed=589824, transcendentals=0),
        compiler_params=PARAMS,
        name="pack",
    )(*terms)


def scan_kernel(_, x_ref, piece_ref, packed_ref, out_ref):
    running = jnp.zeros((8, 512), F32)
    start = x_ref[...].astype(F32)
    for section in range(piece_ref.shape[0]):
        running = running + piece_ref[section].astype(F32)
        out_ref[section, :, :512] = (start + running).astype(BF16)
        out_ref[section, :, 512:] = packed_ref[section]


def scan(index, x_in, pieces, packed):
    return pl.pallas_call(
        scan_kernel,
        out_shape=jax.ShapeDtypeStruct((32, 8, 768), BF16),
        grid_spec=pltpu.PrefetchScalarGridSpec(
            num_scalar_prefetch=1,
            grid=(1,),
            in_specs=[
                pl.BlockSpec((8, 512), lambda i, s: (s[0] // 2, s[0] % 2)),
                pl.BlockSpec((32, 8, 512), lambda i, s: (0, 0, 0)),
                pl.BlockSpec((32, 8, 256), lambda i, s: (0, 0, 0)),
            ],
            out_specs=pl.BlockSpec((32, 8, 768), lambda i, s: (0, 0, 0)),
        ),
        cost_estimate=pl.CostEstimate(flops=262144, bytes_accessed=786432, transcendentals=0),
        compiler_params=PARAMS,
        name="scan",
    )(index, x_in, pieces, packed)


def finish_kernel(in_ref, states_ref, grad_ref):
    for block in range(16):
        for half in range(2):
            states_ref[0, block * 8 : (block + 1) * 8, half * 512 : (half + 1) * 512] = in_ref[
                2 * block + half, :, :512
            ]
    total = in_ref[0, :, 512:].astype(F32)
    for section in range(1, in_ref.shape[0]):
        total = total + in_ref[section, :, 512:].astype(F32)
    for chunk in range(7):
        for row in range(2):
            grad_ref[row : row + 1, chunk * 128 : (chunk + 1) * 128] = total[
                chunk : chunk + 1, row * 128 : (row + 1) * 128
            ]


def finish(arrived):
    shapes = [((1, 128, 1024), BF16), ((2, 896), F32)]
    return pl.pallas_call(
        finish_kernel,
        out_shape=[jax.ShapeDtypeStruct(*s) for s in shapes],
        in_specs=[whole(arrived.shape)],
        out_specs=[whole(s[0]) for s in shapes],
        cost_estimate=pl.CostEstimate(flops=131072, bytes_accessed=786432, transcendentals=0),
        compiler_params=PARAMS,
        name="finish",
    )(arrived)


def gathered_sum(value, keep=None):
    parts = [swap(value, X, k) for k in (1, 2, 3)]
    total = value.astype(F32) if keep is None else keep
    return total + sum(p.astype(F32) for p in parts)


def step(
    x_in,
    neighbour_ids,
    embed_table,
    enc_gate,
    enc_up,
    enc_down,
    query_weight,
    key_weight,
    value_weight,
    out_weight,
    state_grad,
):
    sections = lax.axis_size(SEGMENT)
    section = lax.axis_index(SEGMENT).astype(jnp.int32)
    tensor = lax.axis_index(TENSOR).astype(jnp.int32)
    core = lax.axis_index(C)
    x_index = lax.axis_index(X).astype(jnp.int32)[None]
    t_index = tensor[None]
    s_index = section[None]
    vocab_rows, depth = embed_table.shape
    first_row = (section * lax.axis_size(TENSOR) + tensor) * vocab_rows

    found, passed = lookup(jnp.stack([core.astype(jnp.int32), first_row]), neighbour_ids[None], embed_table)
    paired = (found + swap(passed, C, 1)).reshape(sections, 8, depth)
    w_query, w_key, w_value, w_out = query_weight[0], key_weight[0], value_weight[0], out_weight[0]
    grad_local = state_grad[0]
    own = lax.all_to_all(paired, SEGMENT, 0, 0, tiled=True)
    sent = project(t_index, x_in, w_query, grad_local, w_out, 1)
    sent = swap(sent, C, 1)
    kept = project(t_index, x_in, w_query, grad_local, w_out, 0)
    both = (kept.astype(F32) + sent.astype(F32)).astype(BF16)
    own, both = lax.optimization_barrier((own, both))
    pieces = [both[0]] + [swap(both[k], X, k) for k in (1, 2, 3)]
    heads = sum(p.astype(F32) for p in pieces)

    own = jnp.sum(own.astype(F32), axis=0).astype(BF16)
    own = gathered_sum(own).astype(BF16)
    keep, send = encode(own, swap(own, C, 1), enc_gate, enc_up, enc_down)
    partial = (keep + swap(send, C, 1).astype(F32)).astype(BF16)
    resid = own.astype(F32) + gathered_sum(partial)
    encoding = (
        resid * lax.rsqrt(jnp.mean(resid * resid, axis=-1, keepdims=True) + EPSILON)
    ).astype(BF16)
    enc_own = lax.all_to_all(
        jnp.broadcast_to(encoding[None], (sections, 8, depth)), SEGMENT, 0, 0, tiled=True
    )
    enc_own = enc_own.reshape(2, 128, depth)
    enc_oth = swap(enc_own, C, 1)

    att, *saved = attend(enc_own, enc_oth, w_key, w_value, heads)
    atts = jnp.stack([att] + [swap(att, X, k) for k in (1, 2, 3)])
    keep, send = backward(x_index, heads, saved, w_key, w_value)
    atts_other = swap(atts, C, 1)
    first = output(t_index, atts, w_out, None)
    contribution = output(t_index, atts_other, w_out, first)
    contributions = lax.all_to_all(contribution, SEGMENT, 0, 0, tiled=True)
    terms = (keep.astype(F32) + swap(send, C, 1).astype(F32)).astype(BF16).reshape(4, 64, depth)
    packed = pack([terms[0]] + [swap(terms[k], X, k) for k in (1, 2, 3)])
    mixed = lax.all_to_all(scan(s_index, x_in, contributions, packed), SEGMENT, 0, 0, tiled=True)
    states, enc_grad = finish(mixed)
    return states, enc_grad


def solution(mesh):
    split = Mesh(mesh.devices.reshape(8, 4, 4, 2), SEGMENT_TENSOR)
    return jax.shard_map(
        step,
        mesh=split,
        in_specs=(
            P(None, TENSOR),
            P(),
            P(SEGMENT_TENSOR, None),
            P(None, TENSOR),
            P(None, TENSOR),
            P(TENSOR, None),
            P(SEGMENT, TENSOR, None),
            P(SEGMENT, None, TENSOR),
            P(SEGMENT, None, TENSOR),
            P(SEGMENT, None, TENSOR),
            P(SEGMENT, None, TENSOR),
        ),
        out_specs=(P(SEGMENT, None, TENSOR), P(SEGMENT_TENSOR, None)),
        check_vma=False,
    )
```

```python
import functools
import math

import jax
import jax.numpy as jnp
from jax import lax
from jax.experimental import pallas as pl
from jax.experimental.pallas import tpu as pltpu
from jax.sharding import Mesh
from jax.sharding import PartitionSpec as P


HD = 64
SPAN = 64
Z, Y, X, C = "segment_0", "segment_1", "tensor_0", "tensor_1"
SEGMENT = (Z, Y)
TENSOR = (X, C)
SEGMENT_TENSOR = (Z, Y, X, C)

EPSILON = 1e-06
SCORE_GAIN = 2.0
F32 = jnp.float32
BF16 = jnp.bfloat16


NT = (((1,), (1,)), ((), ()))
TN = (((0,), (0,)), ((), ()))
NN = (((1,), (0,)), ((), ()))

PARAMS = pltpu.CompilerParams(vmem_limit_bytes=24 << 20)


def swap(value, axis, k):
    size = lax.axis_size(axis)
    return lax.ppermute(value, axis, [(i, i ^ k) for i in range(size)])


def dot(lhs, rhs, dims=NN):
    return lax.dot_general(lhs, rhs, dims, preferred_element_type=F32)


def halves(value):
    high = value.astype(BF16)
    return high, (value - high.astype(F32)).astype(BF16)


def head_of(shape, dim):
    return lax.broadcasted_iota(jnp.int32, shape, dim) // HD


def head_mean(value):
    width = value.shape[-1]
    same = head_of((width, width), 0) == head_of((width, width), 1)
    mean = jnp.where(same, 1.0 / HD, 0.0).astype(BF16)
    high, low = halves(value)
    return dot(high, mean) + dot(low, mean)


def by_head(rows):
    heads = rows.shape[-1] // HD
    which = head_of(rows.shape, 1)
    return jnp.concatenate([jnp.where(which == h, rows, 0.0) for h in range(heads)], axis=0)


def project_kernel(index_ref, x_hbm, wq_ref, grad_hbm, wo_ref, send_ref, keep_ref,
                   x_ref, grad_ref, q_buf, o_buf, acc_ref, out_buf, sem):
    starts, outs, ins, back = [], [], [], []
    small = [
        pltpu.make_async_copy(x_hbm, x_ref, sem.at[12]),
        pltpu.make_async_copy(grad_hbm, grad_ref, sem.at[13]),
    ]
    for part in range(4):
        rows = slice(part * 256, (part + 1) * 256)
        ins.append(pltpu.make_async_copy(wq_ref.at[rows, :], q_buf.at[part], sem.at[8 + part]))
    for k in range(8):
        start = pl.multiple_of((index_ref[0] ^ (2 * (k % 4) + 1 - k // 4)) * 256, 256)
        starts.append(start)
        outs.append(pltpu.make_async_copy(wo_ref.at[pl.ds(start, 256), :], o_buf.at[k], sem.at[k]))
        out_ref = keep_ref if k // 4 else send_ref
        back.append(pltpu.make_async_copy(out_buf.at[k], out_ref.at[k % 4], sem.at[14 + k]))
    for copy in small + ins + outs:
        copy.start()
    small[0].wait()
    for part in range(4):
        ins[part].wait()
        rows = x_ref[:, part * 256 : (part + 1) * 256]
        for column in range(4):
            lanes = slice(column * 512, (column + 1) * 512)
            added = dot(rows, q_buf[part, :, lanes])
            acc_ref[:, lanes] = added if part == 0 else acc_ref[:, lanes] + added
    small[1].wait()
    for k in range(8):
        out_buf[k, 0] = acc_ref[:, pl.ds(starts[k], 256)].astype(BF16)
        outs[k].wait()
        out_buf[k, 1] = dot(grad_ref[...], o_buf[k], NT).astype(BF16)
        back[k].start()
    for copy in back:
        copy.wait()


def project(index, x_in, w_query, grad, w_out):
    tokens, depth = x_in.shape
    shape = (4, 2, tokens, 256)
    far = pl.BlockSpec(memory_space=pltpu.HBM)
    return pl.pallas_call(
        project_kernel,
        out_shape=[jax.ShapeDtypeStruct(shape, BF16)] * 2,
        in_specs=[pl.BlockSpec(memory_space=pltpu.SMEM)] + [far] * 4,
        out_specs=[far] * 2,
        scratch_shapes=[
            pltpu.VMEM(x_in.shape, BF16),
            pltpu.VMEM(grad.shape, BF16),
            pltpu.VMEM((4, 256, w_query.shape[1]), BF16),
            pltpu.VMEM((8, 256, depth), BF16),
            pltpu.VMEM((tokens, w_query.shape[1]), F32),
            pltpu.VMEM((8, 2, tokens, 256), BF16),
            pltpu.SemaphoreType.DMA((22,)),
        ],
        cost_estimate=pl.CostEstimate(
            flops=32 * tokens * depth * 256, bytes_accessed=32 * depth * 256, transcendentals=0
        ),
        compiler_params=pltpu.CompilerParams(vmem_limit_bytes=60 << 20),
        name="project",
    )(index, x_in, w_query, grad, w_out)


def attend_kernel(own_ref, oth_ref, order_ref, wk_ref, wv_ref, heads_ref, att_ref,
                  key_ref, val_ref, weight_ref, qhat_ref):
    wk = wk_ref[...]
    wv = wv_ref[...]
    query = heads_ref[0]
    query = query * lax.rsqrt(head_mean(query * query) + EPSILON)
    qhat_ref[...] = query.astype(BF16)
    for span in range(2):
        places = slice(span * 256, (span + 1) * 256)
        enc = dot(order_ref[:256, places], own_ref[...], TN)
        enc = (enc + dot(order_ref[256:, places], oth_ref[...], TN)).astype(BF16)
        key = dot(enc, wk)
        value = dot(enc, wv).astype(BF16)
        key_ref[span] = key
        val_ref[span] = value
        khat = key * lax.rsqrt(head_mean(key * key) + EPSILON)
        q_high, q_low = halves(by_head(query[span * SPAN : (span + 1) * SPAN]))
        k_high, k_low = halves(khat)
        score = dot(q_high, k_high, NT) + dot(q_high, k_low, NT) + dot(q_low, k_high, NT)
        weight = jnp.exp(score * (SCORE_GAIN / math.sqrt(HD)))
        weight = weight / jnp.sum(weight, axis=-1, keepdims=True)
        weight_ref[span] = weight
        mixed = dot(weight.astype(BF16), value)
        which = head_of((SPAN, 256), 1)
        out = jnp.zeros((SPAN, 256), F32)
        for h in range(4):
            out = jnp.where(which == h, mixed[h * SPAN : (h + 1) * SPAN], out)
        att_ref[span * SPAN : (span + 1) * SPAN] = out.astype(BF16)


def whole(shape):
    return pl.BlockSpec(shape, lambda: (0,) * len(shape))


def attend(own, oth, places, w_key, w_value, heads):
    depth = w_key.shape[0]
    piece = whole((2, 128, 256))
    shapes = [((128, 256), BF16), ((2, 256, 256), F32), ((2, 256, 256), BF16),
              ((2, 256, 256), F32), ((128, 256), BF16)]
    return pl.pallas_call(
        attend_kernel,
        out_shape=[jax.ShapeDtypeStruct(*s) for s in shapes],
        in_specs=[whole((256, depth))] * 2 + [whole((512, 512))] + [whole((depth, 256))] * 2 + [piece],
        out_specs=[whole(s[0]) for s in shapes],
        cost_estimate=pl.CostEstimate(
            flops=4 * 512 * depth * 256, bytes_accessed=4 * 512 * depth, transcendentals=131072
        ),
        compiler_params=PARAMS,
        name="attend",
    )(own, oth, places, w_key, w_value, heads)


def backward_kernel(x_ref, heads_ref, key_ref, val_ref, weight_ref, qhat_ref, wk_ref, wv_ref,
                    keep_ref, send_ref):
    wk = wk_ref[...]
    wv = wv_ref[...]
    grad = heads_ref[1]
    for span in range(2):
        rows = slice(span * SPAN, (span + 1) * SPAN)
        d_out = by_head(grad[rows]).astype(BF16)
        q_rows = by_head(qhat_ref[rows].astype(F32)).astype(BF16)
        weight = weight_ref[span]
        value = val_ref[span]
        d_value = dot(weight.astype(BF16), d_out, TN).astype(BF16)
        d_weight = dot(d_out, value, NT)
        d_score = weight * (d_weight - jnp.sum(weight * d_weight, axis=-1, keepdims=True))
        d_khat = dot(d_score.astype(BF16), q_rows, TN) * (SCORE_GAIN / math.sqrt(HD))
        key = key_ref[span]
        scale = lax.rsqrt(head_mean(key * key) + EPSILON)
        khat = key * scale
        d_key = (scale * (d_khat - khat * head_mean(d_khat * khat))).astype(BF16)
        term = dot(d_key, wk, NT) + dot(d_value, wv, NT)
        for block in range(4):
            place = x_ref[0] ^ block
            keep_ref[place, span] = term[block * 32 : (block + 1) * 32].astype(BF16)
            send_ref[place, span] = term[128 + block * 32 : 128 + (block + 1) * 32].astype(BF16)


def backward(x_index, heads, saved, w_key, w_value):
    depth = w_key.shape[0]
    piece = whole((2, 128, 256))
    key, value, weight, qhat = saved
    return pl.pallas_call(
        backward_kernel,
        out_shape=[jax.ShapeDtypeStruct((4, 2, 32, depth), BF16)] * 2,
        in_specs=[pl.BlockSpec(memory_space=pltpu.SMEM)] + [piece]
        + [whole((2, 256, 256))] * 3 + [whole((128, 256))] + [whole((depth, 256))] * 2,
        out_specs=[whole((4, 2, 32, depth))] * 2,
        cost_estimate=pl.CostEstimate(
            flops=4 * 512 * depth * 256, bytes_accessed=4 * 512 * depth, transcendentals=0
        ),
        compiler_params=PARAMS,
        name="backward",
    )(x_index, heads, key, value, weight, qhat, w_key, w_value)


def output_kernel(index_ref, att_ref, wo_ref, *refs, other_core):
    base_ref = refs[0] if other_core else None
    out_ref, buf_ref, sem = refs[-3:]
    copies = []
    for k in range(4):
        row = pl.multiple_of((index_ref[0] ^ (2 * k + other_core)) * 256, 256)
        copies.append(
            pltpu.make_async_copy(
                wo_ref.at[pl.ds(row, 256), :], buf_ref.at[pl.ds(k * 256, 256), :], sem.at[k]
            )
        )
        copies[k].start()
    att = jnp.concatenate([att_ref[k] for k in range(4)], axis=1)
    for copy in copies:
        copy.wait()
    for column in range(4):
        lanes = slice(column * 256, (column + 1) * 256)
        part = dot(att, buf_ref[:, lanes])
        if not other_core:
            out_ref[:, lanes] = part
            continue
        part = (base_ref[:, lanes] + part).astype(BF16)
        half, lane = divmod(column * 256, 512)
        for block in range(16):
            out_ref[2 * block + half, :, lane : lane + 256] = part[block * 8 : (block + 1) * 8]


def output(index, att, w_out, base):
    width = w_out.shape[1]
    second = base is not None
    shape, dtype = ((32, 8, 512), BF16) if second else ((128, width), F32)
    return pl.pallas_call(
        functools.partial(output_kernel, other_core=int(second)),
        out_shape=jax.ShapeDtypeStruct(shape, dtype),
        in_specs=[
            pl.BlockSpec(memory_space=pltpu.SMEM),
            whole((4, 128, 256)),
            pl.BlockSpec(memory_space=pl.ANY),
        ]
        + ([whole((128, width))] if second else []),
        out_specs=whole(shape),
        scratch_shapes=[pltpu.VMEM((1024, width), BF16), pltpu.SemaphoreType.DMA((4,))],
        cost_estimate=pl.CostEstimate(
            flops=2 * 128 * 1024 * width, bytes_accessed=2 * 1024 * width, transcendentals=0
        ),
        compiler_params=PARAMS,
        name="output",
    )(index, att, w_out, *([base] if second else []))


def one_hot(condition):
    return jnp.where(condition, 1.0, 0.0)


def lookup_kernel(index_ref, ids_ref, table_ref, out_ref, sel_ref, idx_ref, over_ref, table_buf, wide_ref, sem):
    copy = pltpu.make_async_copy(table_ref, table_buf, sem)
    copy.start()
    core, first_row, section, x = (index_ref[i] for i in range(4))
    ids = ids_ref[...]
    depth, count = table_ref.shape[0], ids.shape[1]
    left = lax.broadcasted_iota(jnp.int32, (count, count), 0)
    right = lax.broadcasted_iota(jnp.int32, (count, count), 1)

    def columns(row):
        part = jnp.transpose(jnp.broadcast_to(row, (128, count)))
        return jnp.concatenate([part] * (count // 128), axis=1)

    ids_row = ids.astype(F32)
    ids_col = columns(ids_row)
    less = (ids_col < ids_row) | ((ids_col == ids_row) & (left < right))
    rank_row = jnp.sum(one_hot(less), axis=0, keepdims=True)
    rank = rank_row.astype(jnp.int32)
    rank_col = columns(rank_row)[:, :128].astype(jnp.int32)

    shard = lax.broadcasted_iota(jnp.int32, (256, count), 0)
    most = jnp.max(jnp.sum(one_hot((ids >> 8) == shard), axis=1, keepdims=True), axis=0, keepdims=True)
    over = most > 64.0
    over_ref[...] = jnp.broadcast_to(jnp.where(over, 1, 0), over_ref.shape)

    hot = one_hot(lax.broadcasted_iota(jnp.int32, (depth, count), 0) == ids - first_row).astype(BF16)
    lane = lax.broadcasted_iota(jnp.int32, (count, 128), 1)
    block = 2 * (lane & 31) + jnp.where(lane < 32, core, 1 - core)
    pick = one_hot((rank_col & 63) == block).astype(BF16)
    picked = dot(hot, pick).astype(BF16)

    turn = lax.broadcasted_iota(jnp.int32, (16, count), 0)
    slot = (turn & 7) * 64 + 2 * section + jnp.where(turn < 8, core, 1 - core)
    owner = jnp.sum(jnp.where(rank == slot, ids_row, 0.0), axis=1, keepdims=True).astype(jnp.int32)
    source = lax.broadcasted_iota(jnp.int32, (16, 128), 1)
    here = (source == (owner >> 11)) & (((owner >> 8) & 7) == 2 * x + core) & (most <= 64.0)
    sel_ref[...] = one_hot(here).astype(BF16)
    block = rank & 63
    idx_ref[...] = ((block & 1) ^ core) * 256 + (block >> 1) * 8 + (rank >> 6)

    copy.wait()
    rows = dot(picked, table_buf[...], TN)
    wide_ref[...] = jnp.zeros_like(wide_ref)
    for chunk in range(7):
        lanes = slice(chunk * 128, (chunk + 1) * 128)
        wide_ref[:, chunk, :] = rows[:32, lanes]
        wide_ref[:, 8 + chunk, :] = rows[32:64, lanes]
    out_ref[...] = wide_ref[...].astype(BF16)


def lookup(index, ids, table):
    shapes = [((32, 16, 128), BF16), ((16, 128), BF16), (ids.shape, jnp.int32), ((8, 128), jnp.int32)]
    return pl.pallas_call(
        lookup_kernel,
        out_shape=[jax.ShapeDtypeStruct(*s) for s in shapes],
        in_specs=[
            pl.BlockSpec(memory_space=pltpu.SMEM),
            whole(ids.shape),
            pl.BlockSpec(memory_space=pltpu.HBM),
        ],
        out_specs=[whole(s[0]) for s in shapes],
        scratch_shapes=[
            pltpu.VMEM(table.shape, BF16),
            pltpu.VMEM((32, 16, 128), F32),
            pltpu.SemaphoreType.DMA,
        ],
        cost_estimate=pl.CostEstimate(
            flops=2 * 128 * 256 * 896, bytes_accessed=2 * 256 * 896, transcendentals=0
        ),
        compiler_params=PARAMS,
        name="lookup",
    )(index, ids, table)


def place_kernel(sel_ref, piece_ref, out_ref, wide_ref):
    wide_ref[...] = piece_ref[...].astype(F32)
    sel = sel_ref[:, :32]
    for chunk in range(7):
        lanes = slice(chunk * 128, (chunk + 1) * 128)
        for half in range(2):
            slots = slice(half * 8, half * 8 + 8)
            rows = dot(sel[slots], wide_ref[:, half * 8 + chunk, :].astype(BF16))
            out_ref[slots, lanes] = rows.astype(BF16)


def place(sel, pieces):
    shape = (sel.shape[0], 896)
    return pl.pallas_call(
        place_kernel,
        out_shape=jax.ShapeDtypeStruct(shape, BF16),
        in_specs=[whole(sel.shape), whole(pieces.shape)],
        out_specs=whole(shape),
        scratch_shapes=[pltpu.VMEM(pieces.shape, F32)],
        cost_estimate=pl.CostEstimate(flops=917504, bytes_accessed=172032, transcendentals=0),
        compiler_params=PARAMS,
        name="place",
    )(sel, pieces)


def order_kernel(index_ref, idx_ref, out_ref):
    core = index_ref[0]
    count = idx_ref.shape[1]
    source = lax.broadcasted_iota(jnp.int32, (count, count), 0)
    place = lax.broadcasted_iota(jnp.int32, (count, count), 1)
    kind = ((place >> 7) & 1) ^ core
    token = ((place >> 8) << 8) + (((place >> 1) & 15) << 4) + (((place >> 5) & 3) << 2)
    token = token + 2 * kind + (place & 1)
    found = one_hot(source == idx_ref[...]).astype(BF16)
    out_ref[...] = dot(found, one_hot(source == token).astype(BF16)).astype(BF16)


def order(index, idx):
    shape = (idx.shape[1], idx.shape[1])
    return pl.pallas_call(
        order_kernel,
        out_shape=jax.ShapeDtypeStruct(shape, BF16),
        in_specs=[pl.BlockSpec(memory_space=pltpu.SMEM), whole(idx.shape)],
        out_specs=whole(shape),
        cost_estimate=pl.CostEstimate(flops=2 * 512**3, bytes_accessed=526336, transcendentals=0),
        compiler_params=PARAMS,
        name="order",
    )(index, idx)


def dense_lookup(core, first_row, ids, table):
    count = ids.shape[0]
    tokens = jnp.arange(count, dtype=jnp.int32)
    less = (ids[:, None] < ids[None, :]) | (
        (ids[:, None] == ids[None, :]) & (tokens[:, None] < tokens[None, :])
    )
    rank = jnp.sum(less.astype(jnp.int32), axis=0)
    shape = (32, 8)
    block = 2 * lax.broadcasted_iota(jnp.int32, shape, 0)
    turn = 64 * lax.broadcasted_iota(jnp.int32, shape, 1)
    rows = jnp.arange(table.shape[0], dtype=jnp.int32)

    def rows_of(which):
        wanted = (block + turn + which).reshape(-1, 1)
        chosen = jnp.sum(jnp.where(wanted == rank[None, :], ids[None, :], 0), axis=1)
        hot = (chosen[:, None] - first_row == rows[None, :]).astype(BF16)
        return dot(hot, table).astype(BF16)

    rows = jnp.concatenate(
        [rows_of(which).reshape(*shape, table.shape[1]) for which in (core, 1 - core)], axis=1
    )
    arrived = lax.all_to_all(rows, SEGMENT, 0, 0, tiled=True)
    return gathered_sum(jnp.sum(arrived.astype(F32), axis=0).astype(BF16)).astype(BF16)


def settle_kernel(own_ref, p0, p1, p2, p3, out_ref):
    resid = own_ref[...].astype(F32) + sum(p[...].astype(F32) for p in (p0, p1, p2, p3))
    scale = lax.rsqrt(jnp.mean(resid * resid, axis=-1, keepdims=True) + EPSILON)
    out_ref[...] = jnp.broadcast_to((resid * scale).astype(BF16)[None], out_ref.shape)


def settle(own, parts, copies):
    shape = (copies, *own.shape)
    return pl.pallas_call(
        settle_kernel,
        out_shape=jax.ShapeDtypeStruct(shape, BF16),
        in_specs=[whole(own.shape)] * 5,
        out_specs=whole(shape),
        cost_estimate=pl.CostEstimate(flops=57344, bytes_accessed=458752, transcendentals=8),
        compiler_params=PARAMS,
        name="settle",
    )(own, *parts)


def encode_kernel(rows_ref, gate_ref, up_ref, down_ref, keep_ref, send_ref):
    rows = rows_ref[...]
    gate = dot(rows, gate_ref[...], NT)
    hidden = (gate / (1.0 + jnp.exp(-gate)) * dot(rows, up_ref[...], NT)).astype(BF16)
    partial = dot(hidden, down_ref[...])
    keep_ref[...] = partial[:8]
    send_ref[...] = partial[8:].astype(BF16)


def encode(rows, enc_gate, enc_up, enc_down):
    operands = (rows, enc_gate.T, enc_up.T, enc_down)
    shape = (8, rows.shape[1])
    return pl.pallas_call(
        encode_kernel,
        out_shape=[jax.ShapeDtypeStruct(shape, F32), jax.ShapeDtypeStruct(shape, BF16)],
        in_specs=[whole(o.shape) for o in operands],
        out_specs=[whole(shape)] * 2,
        cost_estimate=pl.CostEstimate(
            flops=6 * 16 * 896 * 448, bytes_accessed=6 * 896 * 448, transcendentals=8192
        ),
        compiler_params=PARAMS,
        name="encode",
    )(*operands)


def pack_kernel(t0, t1, t2, t3, out_ref, term_ref, wide_ref):
    for chunk in range(7):
        lanes = slice(chunk * 128, (chunk + 1) * 128)
        term_ref[chunk] = sum(t[:, lanes].astype(F32) for t in (t0, t1, t2, t3))
    wide_ref[...] = jnp.zeros_like(wide_ref)
    for chunk in range(7):
        for row in range(2):
            wide_ref[:, chunk, row * 128 : (row + 1) * 128] = term_ref[
                chunk, pl.ds(row, 32, stride=2), :
            ]
    out_ref[...] = wide_ref[...].astype(BF16)


def pack(terms):
    shape = (32, 8, 256)
    return pl.pallas_call(
        pack_kernel,
        out_shape=jax.ShapeDtypeStruct(shape, BF16),
        in_specs=[whole((64, 896))] * 4,
        out_specs=whole(shape),
        scratch_shapes=[pltpu.VMEM((7, 64, 128), F32), pltpu.VMEM(shape, F32)],
        cost_estimate=pl.CostEstimate(flops=262144, bytes_accessed=589824, transcendentals=0),
        compiler_params=PARAMS,
        name="pack",
    )(*terms)


def scan_kernel(_, x_ref, piece_ref, packed_ref, out_ref):
    running = jnp.zeros((8, 512), F32)
    start = x_ref[...].astype(F32)
    for section in range(piece_ref.shape[0]):
        running = running + piece_ref[section].astype(F32)
        out_ref[section, :, :512] = (start + running).astype(BF16)
        out_ref[section, :, 512:] = packed_ref[section]


def scan(index, x_in, pieces, packed):
    return pl.pallas_call(
        scan_kernel,
        out_shape=jax.ShapeDtypeStruct((32, 8, 768), BF16),
        grid_spec=pltpu.PrefetchScalarGridSpec(
            num_scalar_prefetch=1,
            grid=(1,),
            in_specs=[
                pl.BlockSpec((8, 512), lambda i, s: (s[0] // 2, s[0] % 2)),
                pl.BlockSpec((32, 8, 512), lambda i, s: (0, 0, 0)),
                pl.BlockSpec((32, 8, 256), lambda i, s: (0, 0, 0)),
            ],
            out_specs=pl.BlockSpec((32, 8, 768), lambda i, s: (0, 0, 0)),
        ),
        cost_estimate=pl.CostEstimate(flops=262144, bytes_accessed=786432, transcendentals=0),
        compiler_params=PARAMS,
        name="scan",
    )(index, x_in, pieces, packed)


def finish_kernel(in_ref, states_ref, grad_ref):
    for block in range(16):
        for half in range(2):
            states_ref[0, block * 8 : (block + 1) * 8, half * 512 : (half + 1) * 512] = in_ref[
                2 * block + half, :, :512
            ]
    total = in_ref[0, :, 512:].astype(F32)
    for section in range(1, in_ref.shape[0]):
        total = total + in_ref[section, :, 512:].astype(F32)
    for chunk in range(7):
        for row in range(2):
            grad_ref[row : row + 1, chunk * 128 : (chunk + 1) * 128] = total[
                chunk : chunk + 1, row * 128 : (row + 1) * 128
            ]


def finish(arrived):
    shapes = [((1, 128, 1024), BF16), ((2, 896), F32)]
    return pl.pallas_call(
        finish_kernel,
        out_shape=[jax.ShapeDtypeStruct(*s) for s in shapes],
        in_specs=[whole(arrived.shape)],
        out_specs=[whole(s[0]) for s in shapes],
        cost_estimate=pl.CostEstimate(flops=131072, bytes_accessed=786432, transcendentals=0),
        compiler_params=PARAMS,
        name="finish",
    )(arrived)


def gathered_sum(value, extra=0.0):
    parts = [swap(value, X, k) for k in (1, 2, 3)]
    return value.astype(F32) + sum(p.astype(F32) for p in parts) + extra


def step(
    x_in,
    neighbour_ids,
    embed_table,
    enc_gate,
    enc_up,
    enc_down,
    query_weight,
    key_weight,
    value_weight,
    out_weight,
    state_grad,
):
    sections = lax.axis_size(SEGMENT)
    section = lax.axis_index(SEGMENT).astype(jnp.int32)
    tensor = lax.axis_index(TENSOR).astype(jnp.int32)
    core = lax.axis_index(C)
    x_index = lax.axis_index(X).astype(jnp.int32)[None]
    t_index = tensor[None]
    s_index = section[None]
    vocab_rows, depth = embed_table.shape
    first_row = (section * lax.axis_size(TENSOR) + tensor) * vocab_rows

    core = core.astype(jnp.int32)
    index = jnp.stack([core, first_row, section, x_index[0]])
    found, sel, idx, over = lookup(index, neighbour_ids[None], embed_table)
    w_query, w_key, w_value, w_out = query_weight[0], key_weight[0], value_weight[0], out_weight[0]
    grad_local = state_grad[0]
    own = lax.all_to_all(found, SEGMENT, 0, 0, tiled=True)
    sent, kept = project(t_index, x_in, w_query, grad_local, w_out)
    dense = lax.cond(
        over[0, 0] > 0,
        lambda ids, table: dense_lookup(core, first_row, ids, table),
        lambda ids, table: jnp.zeros((16, depth), BF16),
        neighbour_ids,
        embed_table,
    )
    sent = swap(sent, C, 1)
    both = (kept.astype(F32) + sent.astype(F32)).astype(BF16)
    pieces = [both[0]] + [swap(both[k], X, k) for k in (1, 2, 3)]
    heads = sum(p.astype(F32) for p in pieces)
    idx, heads = lax.optimization_barrier((idx, heads))
    places = order(core[None], idx)

    rows = gathered_sum(place(sel, own), dense.astype(F32)).astype(BF16)
    rows = rows + swap(jnp.concatenate([rows[8:], rows[:8]], axis=0), C, 1)
    own = rows[:8]
    keep, send = encode(rows, enc_gate, enc_up, enc_down)
    partial = (keep + swap(send, C, 1).astype(F32)).astype(BF16)
    copies = settle(own, [partial] + [swap(partial, X, k) for k in (1, 2, 3)], sections)
    enc_own = lax.all_to_all(copies, SEGMENT, 0, 0, tiled=True)
    enc_own = enc_own.reshape(256, depth)
    enc_oth = swap(enc_own, C, 1)

    att, *saved = attend(enc_own, enc_oth, places, w_key, w_value, heads)
    atts = jnp.stack([att] + [swap(att, X, k) for k in (1, 2, 3)])
    keep, send = backward(x_index, heads, saved, w_key, w_value)
    atts_other = swap(atts, C, 1)
    first = output(t_index, atts, w_out, None)
    contribution = output(t_index, atts_other, w_out, first)
    contributions = lax.all_to_all(contribution, SEGMENT, 0, 0, tiled=True)
    terms = (keep.astype(F32) + swap(send, C, 1).astype(F32)).astype(BF16).reshape(4, 64, depth)
    packed = pack([terms[0]] + [swap(terms[k], X, k) for k in (1, 2, 3)])
    mixed = lax.all_to_all(scan(s_index, x_in, contributions, packed), SEGMENT, 0, 0, tiled=True)
    states, enc_grad = finish(mixed)
    return states, enc_grad


def solution(mesh):
    split = Mesh(mesh.devices.reshape(8, 4, 4, 2), SEGMENT_TENSOR)
    return jax.shard_map(
        step,
        mesh=split,
        in_specs=(
            P(None, TENSOR),
            P(),
            P(SEGMENT_TENSOR, None),
            P(None, TENSOR),
            P(None, TENSOR),
            P(TENSOR, None),
            P(SEGMENT, TENSOR, None),
            P(SEGMENT, None, TENSOR),
            P(SEGMENT, None, TENSOR),
            P(SEGMENT, None, TENSOR),
            P(SEGMENT, None, TENSOR),
        ),
        out_specs=(P(SEGMENT, None, TENSOR), P(SEGMENT_TENSOR, None)),
        check_vma=False,
    )
```

```python
import functools
import math

import jax
import jax.numpy as jnp
from jax import lax
from jax.experimental import pallas as pl
from jax.experimental.pallas import tpu as pltpu
from jax.sharding import Mesh
from jax.sharding import PartitionSpec as P


HD = 64
SPAN = 64
Z, Y, X, C = "segment_0", "segment_1", "tensor_0", "tensor_1"
SEGMENT = (Z, Y)
TENSOR = (X, C)
SEGMENT_TENSOR = (Z, Y, X, C)

EPSILON = 1e-06
SCORE_GAIN = 2.0
F32 = jnp.float32
BF16 = jnp.bfloat16


NT = (((1,), (1,)), ((), ()))
TN = (((0,), (0,)), ((), ()))
NN = (((1,), (0,)), ((), ()))

PARAMS = pltpu.CompilerParams(vmem_limit_bytes=24 << 20)


def swap(value, axis, k):
    size = lax.axis_size(axis)
    return lax.ppermute(value, axis, [(i, i ^ k) for i in range(size)])


def dot(lhs, rhs, dims=NN):
    return lax.dot_general(lhs, rhs, dims, preferred_element_type=F32)


def halves(value):
    high = value.astype(BF16)
    return high, (value - high.astype(F32)).astype(BF16)


def head_of(shape, dim):
    return lax.broadcasted_iota(jnp.int32, shape, dim) // HD


def head_mean(value):
    width = value.shape[-1]
    same = head_of((width, width), 0) == head_of((width, width), 1)
    mean = jnp.where(same, 1.0 / HD, 0.0).astype(BF16)
    high, low = halves(value)
    return dot(high, mean) + dot(low, mean)


def by_head(rows):
    heads = rows.shape[-1] // HD
    which = head_of(rows.shape, 1)
    return jnp.concatenate([jnp.where(which == h, rows, 0.0) for h in range(heads)], axis=0)


def project_kernel(index_ref, x_hbm, wq_ref, grad_hbm, wo_ref, send_ref, keep_ref,
                   x_ref, grad_ref, q_buf, o_buf, acc_ref, out_buf, sem):
    starts, outs, ins, back = [], [], [], []
    small = [
        pltpu.make_async_copy(x_hbm, x_ref, sem.at[12]),
        pltpu.make_async_copy(grad_hbm, grad_ref, sem.at[13]),
    ]
    for part in range(4):
        rows = slice(part * 256, (part + 1) * 256)
        ins.append(pltpu.make_async_copy(wq_ref.at[rows, :], q_buf.at[part], sem.at[8 + part]))
    for k in range(8):
        start = pl.multiple_of((index_ref[0] ^ (2 * (k % 4) + 1 - k // 4)) * 256, 256)
        starts.append(start)
        outs.append(pltpu.make_async_copy(wo_ref.at[pl.ds(start, 256), :], o_buf.at[k], sem.at[k]))
        out_ref = keep_ref if k // 4 else send_ref
        back.append(pltpu.make_async_copy(out_buf.at[k], out_ref.at[k % 4], sem.at[14 + k]))
    for copy in small + ins + outs:
        copy.start()
    small[0].wait()
    for part in range(4):
        ins[part].wait()
        rows = x_ref[:, part * 256 : (part + 1) * 256]
        for column in range(4):
            lanes = slice(column * 512, (column + 1) * 512)
            added = dot(rows, q_buf[part, :, lanes])
            acc_ref[:, lanes] = added if part == 0 else acc_ref[:, lanes] + added
    small[1].wait()
    for k in range(8):
        out_buf[k, 0] = acc_ref[:, pl.ds(starts[k], 256)].astype(BF16)
        outs[k].wait()
        out_buf[k, 1] = dot(grad_ref[...], o_buf[k], NT).astype(BF16)
        back[k].start()
    for copy in back:
        copy.wait()


def project(index, x_in, w_query, grad, w_out):
    tokens, depth = x_in.shape
    shape = (4, 2, tokens, 256)
    far = pl.BlockSpec(memory_space=pltpu.HBM)
    return pl.pallas_call(
        project_kernel,
        out_shape=[jax.ShapeDtypeStruct(shape, BF16)] * 2,
        in_specs=[pl.BlockSpec(memory_space=pltpu.SMEM)] + [far] * 4,
        out_specs=[far] * 2,
        scratch_shapes=[
            pltpu.VMEM(x_in.shape, BF16),
            pltpu.VMEM(grad.shape, BF16),
            pltpu.VMEM((4, 256, w_query.shape[1]), BF16),
            pltpu.VMEM((8, 256, depth), BF16),
            pltpu.VMEM((tokens, w_query.shape[1]), F32),
            pltpu.VMEM((8, 2, tokens, 256), BF16),
            pltpu.SemaphoreType.DMA((22,)),
        ],
        cost_estimate=pl.CostEstimate(
            flops=32 * tokens * depth * 256, bytes_accessed=32 * depth * 256, transcendentals=0
        ),
        compiler_params=pltpu.CompilerParams(vmem_limit_bytes=60 << 20),
        name="project",
    )(index, x_in, w_query, grad, w_out)


def placed_keys(rows_ref, order, wk_ref, wv_ref):
    rows = rows_ref[...]
    high, low = halves(dot(rows, wk_ref[...]))
    value = dot(rows, wv_ref[...]).astype(BF16)
    return dot(order, high, TN) + dot(order, low, TN), dot(order, value, TN)


def attend_own_kernel(own_ref, order_ref, wk_ref, wv_ref, heads_ref, key_ref, val_ref, qhat_ref):
    key_ref[...], val_ref[...] = placed_keys(own_ref, order_ref[:256, :], wk_ref, wv_ref)
    query = heads_ref[0]
    qhat_ref[...] = query * lax.rsqrt(head_mean(query * query) + EPSILON)


def attend_kernel(oth_ref, order_ref, wk_ref, wv_ref, part_k_ref, part_v_ref, qhat_ref,
                  att_ref, key_ref, val_ref, weight_ref):
    keys, values = placed_keys(oth_ref, order_ref[256:, :], wk_ref, wv_ref)
    keys = keys + part_k_ref[...]
    values = (values + part_v_ref[...]).astype(BF16)
    query = qhat_ref[...]
    for span in range(2):
        key = keys[span * 256 : (span + 1) * 256]
        value = values[span * 256 : (span + 1) * 256]
        key_ref[span] = key
        val_ref[span] = value
        khat = key * lax.rsqrt(head_mean(key * key) + EPSILON)
        q_high, q_low = halves(by_head(query[span * SPAN : (span + 1) * SPAN]))
        k_high, k_low = halves(khat)
        score = dot(q_high, k_high, NT) + dot(q_high, k_low, NT) + dot(q_low, k_high, NT)
        weight = jnp.exp(score * (SCORE_GAIN / math.sqrt(HD)))
        weight = weight / jnp.sum(weight, axis=-1, keepdims=True)
        weight_ref[span] = weight
        mixed = dot(weight.astype(BF16), value)
        which = head_of((SPAN, 256), 1)
        out = jnp.zeros((SPAN, 256), F32)
        for h in range(4):
            out = jnp.where(which == h, mixed[h * SPAN : (h + 1) * SPAN], out)
        att_ref[span * SPAN : (span + 1) * SPAN] = out.astype(BF16)


def whole(shape):
    return pl.BlockSpec(shape, lambda: (0,) * len(shape))


def attend_own(own, places, w_key, w_value, heads):
    operands = (own, places, w_key, w_value, heads)
    shapes = [((512, 256), F32), ((512, 256), F32), ((128, 256), F32)]
    return pl.pallas_call(
        attend_own_kernel,
        out_shape=[jax.ShapeDtypeStruct(*s) for s in shapes],
        in_specs=[whole(o.shape) for o in operands],
        out_specs=[whole(s[0]) for s in shapes],
        cost_estimate=pl.CostEstimate(
            flops=4 * 256 * 896 * 256, bytes_accessed=4 * 512 * 896, transcendentals=128
        ),
        compiler_params=PARAMS,
        name="attend_own",
    )(*operands)


def attend(oth, places, w_key, w_value, part_k, part_v, qhat):
    operands = (oth, places, w_key, w_value, part_k, part_v, qhat)
    shapes = [((128, 256), BF16), ((2, 256, 256), F32), ((2, 256, 256), BF16), ((2, 256, 256), F32)]
    return pl.pallas_call(
        attend_kernel,
        out_shape=[jax.ShapeDtypeStruct(*s) for s in shapes],
        in_specs=[whole(o.shape) for o in operands],
        out_specs=[whole(s[0]) for s in shapes],
        cost_estimate=pl.CostEstimate(
            flops=4 * 512 * 896 * 256, bytes_accessed=4 * 512 * 896, transcendentals=131072
        ),
        compiler_params=PARAMS,
        name="attend",
    )(*operands)


def backward_kernel(x_ref, heads_ref, key_ref, val_ref, weight_ref, qhat_ref, wk_ref, wv_ref,
                    keep_ref, send_ref):
    wk = wk_ref[...]
    wv = wv_ref[...]
    grad = heads_ref[1]
    for span in range(2):
        rows = slice(span * SPAN, (span + 1) * SPAN)
        d_out = by_head(grad[rows]).astype(BF16)
        q_rows = by_head(qhat_ref[rows]).astype(BF16)
        weight = weight_ref[span]
        value = val_ref[span]
        d_value = dot(weight.astype(BF16), d_out, TN).astype(BF16)
        d_weight = dot(d_out, value, NT)
        d_score = weight * (d_weight - jnp.sum(weight * d_weight, axis=-1, keepdims=True))
        d_khat = dot(d_score.astype(BF16), q_rows, TN) * (SCORE_GAIN / math.sqrt(HD))
        key = key_ref[span]
        scale = lax.rsqrt(head_mean(key * key) + EPSILON)
        khat = key * scale
        d_key = (scale * (d_khat - khat * head_mean(d_khat * khat))).astype(BF16)
        term = dot(d_key, wk, NT) + dot(d_value, wv, NT)
        for block in range(4):
            place = x_ref[0] ^ block
            keep_ref[place, span] = term[block * 32 : (block + 1) * 32].astype(BF16)
            send_ref[place, span] = term[128 + block * 32 : 128 + (block + 1) * 32].astype(BF16)


def backward(x_index, heads, saved, w_key, w_value):
    depth = w_key.shape[0]
    piece = whole((2, 128, 256))
    key, value, weight, qhat = saved
    return pl.pallas_call(
        backward_kernel,
        out_shape=[jax.ShapeDtypeStruct((4, 2, 32, depth), BF16)] * 2,
        in_specs=[pl.BlockSpec(memory_space=pltpu.SMEM)] + [piece]
        + [whole((2, 256, 256))] * 3 + [whole((128, 256))] + [whole((depth, 256))] * 2,
        out_specs=[whole((4, 2, 32, depth))] * 2,
        cost_estimate=pl.CostEstimate(
            flops=4 * 512 * depth * 256, bytes_accessed=4 * 512 * depth, transcendentals=0
        ),
        compiler_params=PARAMS,
        name="backward",
    )(x_index, heads, key, value, weight, qhat, w_key, w_value)


def output_kernel(index_ref, att_ref, wo_ref, *refs, other_core):
    base_ref = refs[0] if other_core else None
    out_ref, buf_ref, sem = refs[-3:]
    copies = []
    for k in range(4):
        row = pl.multiple_of((index_ref[0] ^ (2 * k + other_core)) * 256, 256)
        copies.append(
            pltpu.make_async_copy(
                wo_ref.at[pl.ds(row, 256), :], buf_ref.at[pl.ds(k * 256, 256), :], sem.at[k]
            )
        )
        copies[k].start()
    att = jnp.concatenate([att_ref[k] for k in range(4)], axis=1)
    for copy in copies:
        copy.wait()
    for column in range(4):
        lanes = slice(column * 256, (column + 1) * 256)
        part = dot(att, buf_ref[:, lanes])
        if not other_core:
            out_ref[:, lanes] = part
            continue
        part = (base_ref[:, lanes] + part).astype(BF16)
        half, lane = divmod(column * 256, 512)
        for block in range(16):
            out_ref[2 * block + half, :, lane : lane + 256] = part[block * 8 : (block + 1) * 8]


def output(index, att, w_out, base):
    width = w_out.shape[1]
    second = base is not None
    shape, dtype = ((32, 8, 512), BF16) if second else ((128, width), F32)
    return pl.pallas_call(
        functools.partial(output_kernel, other_core=int(second)),
        out_shape=jax.ShapeDtypeStruct(shape, dtype),
        in_specs=[
            pl.BlockSpec(memory_space=pltpu.SMEM),
            whole((4, 128, 256)),
            pl.BlockSpec(memory_space=pl.ANY),
        ]
        + ([whole((128, width))] if second else []),
        out_specs=whole(shape),
        scratch_shapes=[pltpu.VMEM((1024, width), BF16), pltpu.SemaphoreType.DMA((4,))],
        cost_estimate=pl.CostEstimate(
            flops=2 * 128 * 1024 * width, bytes_accessed=2 * 1024 * width, transcendentals=0
        ),
        compiler_params=PARAMS,
        name="output",
    )(index, att, w_out, *([base] if second else []))


def one_hot(condition):
    return jnp.where(condition, 1.0, 0.0)


def lookup_kernel(index_ref, ids_ref, table_ref, out_ref, sel_ref, idx_ref, over_ref, table_buf, wide_ref, sem):
    copy = pltpu.make_async_copy(table_ref, table_buf, sem)
    copy.start()
    core, first_row, section, x = (index_ref[i] for i in range(4))
    ids = ids_ref[...]
    depth, count = table_ref.shape[0], ids.shape[1]
    left = lax.broadcasted_iota(jnp.int32, (count, count), 0)
    right = lax.broadcasted_iota(jnp.int32, (count, count), 1)

    def columns(row):
        part = jnp.transpose(jnp.broadcast_to(row, (128, count)))
        return jnp.concatenate([part] * (count // 128), axis=1)

    ids_row = ids.astype(F32)
    ids_col = columns(ids_row)
    less = (ids_col < ids_row) | ((ids_col == ids_row) & (left < right))
    rank_row = jnp.sum(one_hot(less), axis=0, keepdims=True)
    rank = rank_row.astype(jnp.int32)
    rank_col = columns(rank_row)[:, :128].astype(jnp.int32)

    shard = lax.broadcasted_iota(jnp.int32, (256, count), 0)
    most = jnp.max(jnp.sum(one_hot((ids >> 8) == shard), axis=1, keepdims=True), axis=0, keepdims=True)
    over = most > 64.0
    over_ref[...] = jnp.broadcast_to(jnp.where(over, 1, 0), over_ref.shape)

    hot = one_hot(lax.broadcasted_iota(jnp.int32, (depth, count), 0) == ids - first_row).astype(BF16)
    lane = lax.broadcasted_iota(jnp.int32, (count, 128), 1)
    block = 2 * (lane & 31) + jnp.where(lane < 32, core, 1 - core)
    pick = one_hot((rank_col & 63) == block).astype(BF16)
    picked = dot(hot, pick).astype(BF16)

    turn = lax.broadcasted_iota(jnp.int32, (16, count), 0)
    slot = (turn & 7) * 64 + 2 * section + jnp.where(turn < 8, core, 1 - core)
    owner = jnp.sum(jnp.where(rank == slot, ids_row, 0.0), axis=1, keepdims=True).astype(jnp.int32)
    source = lax.broadcasted_iota(jnp.int32, (16, 128), 1)
    here = (source == (owner >> 11)) & (((owner >> 8) & 7) == 2 * x + core) & (most <= 64.0)
    sel_ref[...] = one_hot(here).astype(BF16)
    block = rank & 63
    idx_ref[...] = ((block & 1) ^ core) * 256 + (block >> 1) * 8 + (rank >> 6)

    copy.wait()
    rows = dot(picked, table_buf[...], TN)
    wide_ref[...] = jnp.zeros_like(wide_ref)
    for chunk in range(7):
        lanes = slice(chunk * 128, (chunk + 1) * 128)
        wide_ref[:, chunk, :] = rows[:32, lanes]
        wide_ref[:, 8 + chunk, :] = rows[32:64, lanes]
    out_ref[...] = wide_ref[...].astype(BF16)


def lookup(index, ids, table):
    shapes = [((32, 16, 128), BF16), ((16, 128), BF16), (ids.shape, jnp.int32), ((8, 128), jnp.int32)]
    return pl.pallas_call(
        lookup_kernel,
        out_shape=[jax.ShapeDtypeStruct(*s) for s in shapes],
        in_specs=[
            pl.BlockSpec(memory_space=pltpu.SMEM),
            whole(ids.shape),
            pl.BlockSpec(memory_space=pltpu.HBM),
        ],
        out_specs=[whole(s[0]) for s in shapes],
        scratch_shapes=[
            pltpu.VMEM(table.shape, BF16),
            pltpu.VMEM((32, 16, 128), F32),
            pltpu.SemaphoreType.DMA,
        ],
        cost_estimate=pl.CostEstimate(
            flops=2 * 128 * 256 * 896, bytes_accessed=2 * 256 * 896, transcendentals=0
        ),
        compiler_params=PARAMS,
        name="lookup",
    )(index, ids, table)


def place_kernel(sel_ref, piece_ref, out_ref, wide_ref):
    wide_ref[...] = piece_ref[...].astype(F32)
    sel = sel_ref[:, :32]
    for chunk in range(7):
        lanes = slice(chunk * 128, (chunk + 1) * 128)
        for half in range(2):
            slots = slice(half * 8, half * 8 + 8)
            rows = dot(sel[slots], wide_ref[:, half * 8 + chunk, :].astype(BF16))
            out_ref[slots, lanes] = rows.astype(BF16)


def place(sel, pieces):
    shape = (sel.shape[0], 896)
    return pl.pallas_call(
        place_kernel,
        out_shape=jax.ShapeDtypeStruct(shape, BF16),
        in_specs=[whole(sel.shape), whole(pieces.shape)],
        out_specs=whole(shape),
        scratch_shapes=[pltpu.VMEM(pieces.shape, F32)],
        cost_estimate=pl.CostEstimate(flops=917504, bytes_accessed=172032, transcendentals=0),
        compiler_params=PARAMS,
        name="place",
    )(sel, pieces)


def order_kernel(index_ref, idx_ref, out_ref):
    core = index_ref[0]
    count = idx_ref.shape[1]
    source = lax.broadcasted_iota(jnp.int32, (count, count), 0)
    place = lax.broadcasted_iota(jnp.int32, (count, count), 1)
    kind = ((place >> 7) & 1) ^ core
    token = ((place >> 8) << 8) + (((place >> 1) & 15) << 4) + (((place >> 5) & 3) << 2)
    token = token + 2 * kind + (place & 1)
    found = one_hot(source == idx_ref[...]).astype(BF16)
    out_ref[...] = dot(found, one_hot(source == token).astype(BF16)).astype(BF16)


def order(index, idx):
    shape = (idx.shape[1], idx.shape[1])
    return pl.pallas_call(
        order_kernel,
        out_shape=jax.ShapeDtypeStruct(shape, BF16),
        in_specs=[pl.BlockSpec(memory_space=pltpu.SMEM), whole(idx.shape)],
        out_specs=whole(shape),
        cost_estimate=pl.CostEstimate(flops=2 * 512**3, bytes_accessed=526336, transcendentals=0),
        compiler_params=PARAMS,
        name="order",
    )(index, idx)


def dense_lookup(core, first_row, ids, table):
    count = ids.shape[0]
    tokens = jnp.arange(count, dtype=jnp.int32)
    less = (ids[:, None] < ids[None, :]) | (
        (ids[:, None] == ids[None, :]) & (tokens[:, None] < tokens[None, :])
    )
    rank = jnp.sum(less.astype(jnp.int32), axis=0)
    shape = (32, 8)
    block = 2 * lax.broadcasted_iota(jnp.int32, shape, 0)
    turn = 64 * lax.broadcasted_iota(jnp.int32, shape, 1)
    rows = jnp.arange(table.shape[0], dtype=jnp.int32)

    def rows_of(which):
        wanted = (block + turn + which).reshape(-1, 1)
        chosen = jnp.sum(jnp.where(wanted == rank[None, :], ids[None, :], 0), axis=1)
        hot = (chosen[:, None] - first_row == rows[None, :]).astype(BF16)
        return dot(hot, table).astype(BF16)

    rows = jnp.concatenate(
        [rows_of(which).reshape(*shape, table.shape[1]) for which in (core, 1 - core)], axis=1
    )
    arrived = lax.all_to_all(rows, SEGMENT, 0, 0, tiled=True)
    return gathered_sum(jnp.sum(arrived.astype(F32), axis=0).astype(BF16)).astype(BF16)


def settle_kernel(own_ref, p0, p1, p2, p3, out_ref):
    resid = own_ref[...].astype(F32) + sum(p[...].astype(F32) for p in (p0, p1, p2, p3))
    scale = lax.rsqrt(jnp.mean(resid * resid, axis=-1, keepdims=True) + EPSILON)
    out_ref[...] = jnp.broadcast_to((resid * scale).astype(BF16)[None], out_ref.shape)


def settle(own, parts, copies):
    shape = (copies, *own.shape)
    return pl.pallas_call(
        settle_kernel,
        out_shape=jax.ShapeDtypeStruct(shape, BF16),
        in_specs=[whole(own.shape)] * 5,
        out_specs=whole(shape),
        cost_estimate=pl.CostEstimate(flops=57344, bytes_accessed=458752, transcendentals=8),
        compiler_params=PARAMS,
        name="settle",
    )(own, *parts)


def encode_kernel(rows_ref, gate_ref, up_ref, down_ref, keep_ref, send_ref):
    rows = rows_ref[...]
    gate = dot(rows, gate_ref[...], NT)
    hidden = (gate / (1.0 + jnp.exp(-gate)) * dot(rows, up_ref[...], NT)).astype(BF16)
    partial = dot(hidden, down_ref[...])
    keep_ref[...] = partial[:8]
    send_ref[...] = partial[8:].astype(BF16)


def encode(rows, enc_gate, enc_up, enc_down):
    operands = (rows, enc_gate.T, enc_up.T, enc_down)
    shape = (8, rows.shape[1])
    return pl.pallas_call(
        encode_kernel,
        out_shape=[jax.ShapeDtypeStruct(shape, F32), jax.ShapeDtypeStruct(shape, BF16)],
        in_specs=[whole(o.shape) for o in operands],
        out_specs=[whole(shape)] * 2,
        cost_estimate=pl.CostEstimate(
            flops=6 * 16 * 896 * 448, bytes_accessed=6 * 896 * 448, transcendentals=8192
        ),
        compiler_params=PARAMS,
        name="encode",
    )(*operands)


def pack_kernel(t0, t1, t2, t3, out_ref, term_ref, wide_ref):
    for chunk in range(7):
        lanes = slice(chunk * 128, (chunk + 1) * 128)
        term_ref[chunk] = sum(t[:, lanes].astype(F32) for t in (t0, t1, t2, t3))
    wide_ref[...] = jnp.zeros_like(wide_ref)
    for chunk in range(7):
        for row in range(2):
            wide_ref[:, chunk, row * 128 : (row + 1) * 128] = term_ref[
                chunk, pl.ds(row, 32, stride=2), :
            ]
    out_ref[...] = wide_ref[...].astype(BF16)


def pack(terms):
    shape = (32, 8, 256)
    return pl.pallas_call(
        pack_kernel,
        out_shape=jax.ShapeDtypeStruct(shape, BF16),
        in_specs=[whole((64, 896))] * 4,
        out_specs=whole(shape),
        scratch_shapes=[pltpu.VMEM((7, 64, 128), F32), pltpu.VMEM(shape, F32)],
        cost_estimate=pl.CostEstimate(flops=262144, bytes_accessed=589824, transcendentals=0),
        compiler_params=PARAMS,
        name="pack",
    )(*terms)


def scan_kernel(_, x_ref, piece_ref, packed_ref, out_ref):
    running = jnp.zeros((8, 512), F32)
    start = x_ref[...].astype(F32)
    for section in range(piece_ref.shape[0]):
        running = running + piece_ref[section].astype(F32)
        out_ref[section, :, :512] = (start + running).astype(BF16)
        out_ref[section, :, 512:] = packed_ref[section]


def scan(index, x_in, pieces, packed):
    return pl.pallas_call(
        scan_kernel,
        out_shape=jax.ShapeDtypeStruct((32, 8, 768), BF16),
        grid_spec=pltpu.PrefetchScalarGridSpec(
            num_scalar_prefetch=1,
            grid=(1,),
            in_specs=[
                pl.BlockSpec((8, 512), lambda i, s: (s[0] // 2, s[0] % 2)),
                pl.BlockSpec((32, 8, 512), lambda i, s: (0, 0, 0)),
                pl.BlockSpec((32, 8, 256), lambda i, s: (0, 0, 0)),
            ],
            out_specs=pl.BlockSpec((32, 8, 768), lambda i, s: (0, 0, 0)),
        ),
        cost_estimate=pl.CostEstimate(flops=262144, bytes_accessed=786432, transcendentals=0),
        compiler_params=PARAMS,
        name="scan",
    )(index, x_in, pieces, packed)


def finish_kernel(in_ref, states_ref, grad_ref):
    for block in range(16):
        for half in range(2):
            states_ref[0, block * 8 : (block + 1) * 8, half * 512 : (half + 1) * 512] = in_ref[
                2 * block + half, :, :512
            ]
    total = in_ref[0, :, 512:].astype(F32)
    for section in range(1, in_ref.shape[0]):
        total = total + in_ref[section, :, 512:].astype(F32)
    for chunk in range(7):
        for row in range(2):
            grad_ref[row : row + 1, chunk * 128 : (chunk + 1) * 128] = total[
                chunk : chunk + 1, row * 128 : (row + 1) * 128
            ]


def finish(arrived):
    shapes = [((1, 128, 1024), BF16), ((2, 896), F32)]
    return pl.pallas_call(
        finish_kernel,
        out_shape=[jax.ShapeDtypeStruct(*s) for s in shapes],
        in_specs=[whole(arrived.shape)],
        out_specs=[whole(s[0]) for s in shapes],
        cost_estimate=pl.CostEstimate(flops=131072, bytes_accessed=786432, transcendentals=0),
        compiler_params=PARAMS,
        name="finish",
    )(arrived)


def gathered_sum(value, extra=0.0):
    parts = [swap(value, X, k) for k in (1, 2, 3)]
    return value.astype(F32) + sum(p.astype(F32) for p in parts) + extra


def step(
    x_in,
    neighbour_ids,
    embed_table,
    enc_gate,
    enc_up,
    enc_down,
    query_weight,
    key_weight,
    value_weight,
    out_weight,
    state_grad,
):
    sections = lax.axis_size(SEGMENT)
    section = lax.axis_index(SEGMENT).astype(jnp.int32)
    tensor = lax.axis_index(TENSOR).astype(jnp.int32)
    core = lax.axis_index(C)
    x_index = lax.axis_index(X).astype(jnp.int32)[None]
    t_index = tensor[None]
    s_index = section[None]
    vocab_rows, depth = embed_table.shape
    first_row = (section * lax.axis_size(TENSOR) + tensor) * vocab_rows

    core = core.astype(jnp.int32)
    index = jnp.stack([core, first_row, section, x_index[0]])
    found, sel, idx, over = lookup(index, neighbour_ids[None], embed_table)
    w_query, w_key, w_value, w_out = query_weight[0], key_weight[0], value_weight[0], out_weight[0]
    grad_local = state_grad[0]
    own = lax.all_to_all(found, SEGMENT, 0, 0, tiled=True)
    sent, kept = project(t_index, x_in, w_query, grad_local, w_out)
    dense = lax.cond(
        over[0, 0] > 0,
        lambda ids, table: dense_lookup(core, first_row, ids, table),
        lambda ids, table: jnp.zeros((16, depth), BF16),
        neighbour_ids,
        embed_table,
    )
    sent = swap(sent, C, 1)
    both = (kept.astype(F32) + sent.astype(F32)).astype(BF16)
    pieces = [both[0]] + [swap(both[k], X, k) for k in (1, 2, 3)]
    heads = sum(p.astype(F32) for p in pieces)
    idx, heads = lax.optimization_barrier((idx, heads))
    places = order(core[None], idx)

    rows = gathered_sum(place(sel, own), dense.astype(F32)).astype(BF16)
    rows = rows + swap(jnp.concatenate([rows[8:], rows[:8]], axis=0), C, 1)
    own = rows[:8]
    keep, send = encode(rows, enc_gate, enc_up, enc_down)
    partial = (keep + swap(send, C, 1).astype(F32)).astype(BF16)
    copies = settle(own, [partial] + [swap(partial, X, k) for k in (1, 2, 3)], sections)
    enc_own = lax.all_to_all(copies, SEGMENT, 0, 0, tiled=True)
    enc_own = enc_own.reshape(256, depth)
    enc_oth = swap(enc_own, C, 1)

    part_k, part_v, qhat = attend_own(enc_own, places, w_key, w_value, heads)
    att, *saved = attend(enc_oth, places, w_key, w_value, part_k, part_v, qhat)
    saved.append(qhat)
    atts = jnp.stack([att] + [swap(att, X, k) for k in (1, 2, 3)])
    keep, send = backward(x_index, heads, saved, w_key, w_value)
    atts_other = swap(atts, C, 1)
    first = output(t_index, atts, w_out, None)
    contribution = output(t_index, atts_other, w_out, first)
    contributions = lax.all_to_all(contribution, SEGMENT, 0, 0, tiled=True)
    terms = (keep.astype(F32) + swap(send, C, 1).astype(F32)).astype(BF16).reshape(4, 64, depth)
    packed = pack([terms[0]] + [swap(terms[k], X, k) for k in (1, 2, 3)])
    mixed = lax.all_to_all(scan(s_index, x_in, contributions, packed), SEGMENT, 0, 0, tiled=True)
    states, enc_grad = finish(mixed)
    return states, enc_grad


def solution(mesh):
    split = Mesh(mesh.devices.reshape(8, 4, 4, 2), SEGMENT_TENSOR)
    return jax.shard_map(
        step,
        mesh=split,
        in_specs=(
            P(None, TENSOR),
            P(),
            P(SEGMENT_TENSOR, None),
            P(None, TENSOR),
            P(None, TENSOR),
            P(TENSOR, None),
            P(SEGMENT, TENSOR, None),
            P(SEGMENT, None, TENSOR),
            P(SEGMENT, None, TENSOR),
            P(SEGMENT, None, TENSOR),
            P(SEGMENT, None, TENSOR),
        ),
        out_specs=(P(SEGMENT, None, TENSOR), P(SEGMENT_TENSOR, None)),
        check_vma=False,
    )
```
